512 devices in a mesh: seq: 64 (over x_lo, z, core), rep: 8 (over y, x_hi).
Axes of the slice: x: 4 (x_hi: 2, x_lo: 2; x = x_hi * 2 + x_lo), y: 4, z: 16, core: 2. Of those that a mesh axis runs over, the one named last changes fastest.
Arguments:
- queries: bfloat16 [8, 8192, 2048], P('rep', 'seq'), may hold values from -9 to 9
- keys: bfloat16 [8, 8192, 512], P('rep', 'seq'), may hold values from -9 to 9
- values: bfloat16 [8, 8192, 512], P('rep', 'seq'), may hold values from -6 to 6
- conv_taps: float32 [4, 512], replicated, may hold values from -2 to 2
- grad_out: bfloat16 [8, 8192, 2048], P('rep', 'seq'), may hold values from -24 to 24
Outputs:
- grad_queries: bfloat16 [8, 8192, 2048], P('rep', 'seq')
- grad_keys: bfloat16 [8, 8192, 512], P('rep', 'seq')
- grad_values: bfloat16 [8, 8192, 512], P('rep', 'seq')
- grad_taps: float32 [2048], P('seq')
The draws below stay inside these ranges and needn't reach their ends.
All inputs are finite; a program needn't handle non-finite values.
Results may differ from the reference program's by a relative error of at most 0.012.
Values may be sent and summed in bfloat16 or wider, within the bound.
A program may use at most 64 MiB of HBM per device.

```python
import math
import jax
import jax.numpy as jnp
from jax import lax

HEAD_SIZE = 128
QUERY_HEADS = 16
KEY_VALUE_HEADS = 4
TAPS = 4
TOK_DEV = 128
WINDOW = 1024
ROLLOUT_COUNT = 8
ROLLOUT_LENGTH = 8192
KVW = 512


def draw_queries(key, part):
    base_key = jax.random.fold_in(key, 11)
    array_shape = (ROLLOUT_COUNT, ROLLOUT_LENGTH, QUERY_HEADS * HEAD_SIZE)
    drawn = jnp.clip(jax.random.normal(base_key, array_shape, jnp.float32), -6.0, 6.0)
    return drawn.astype(jnp.bfloat16)


def draw_keys(key, part):
    base_key = jax.random.fold_in(key, 23)
    array_shape = (ROLLOUT_COUNT, ROLLOUT_LENGTH, KEY_VALUE_HEADS * HEAD_SIZE)
    drawn = jnp.clip(jax.random.normal(base_key, array_shape, jnp.float32), -6.0, 6.0)
    return drawn.astype(jnp.bfloat16)


def draw_grad_out(key, part):
    array_shape = (ROLLOUT_COUNT, ROLLOUT_LENGTH, QUERY_HEADS * HEAD_SIZE)
    noise_key = jax.random.fold_in(key, 31)
    positions = jnp.arange(ROLLOUT_LENGTH).astype(jnp.float32)
    rising = 1.0 + 2.0 * positions / float(ROLLOUT_LENGTH - 1)
    drawn = jnp.clip(jax.random.normal(noise_key, array_shape, jnp.float32), -4.0, 4.0)
    drawn = drawn * rising[None, :, None]
    return jnp.clip(drawn, -24.0, 24.0).astype(jnp.bfloat16)


def level_of(key, shape, shards, least, top_value):
    level = 1.0
    for axis_at, parts in shards:
        steps = jax.random.uniform(jax.random.fold_in(jax.random.fold_in(key, 6), axis_at), (parts,), jnp.float32, least / len(shards), top_value / len(shards))
        level = level * jnp.repeat(jnp.exp(steps), shape[axis_at] // parts).reshape((-1,) + (1,) * (len(shape) - 1 - axis_at))
    return level


def scatter_about(rng, shape, deviation, limit, split=(), held_as=jnp.bfloat16):
    drawn = deviation * jax.random.normal(rng, shape, jnp.float32)
    if split:
        drawn = drawn * level_of(rng, shape, split, -0.22, 0.18)
    return jnp.clip(drawn, -limit, limit).astype(held_as)


def setup_inputs(seed: int = 0) -> dict:
    key_of = jax.random.split(jax.random.key(seed), 6)
    return {
        "queries": draw_queries(jax.random.fold_in(key_of[5], 71), 0),
        "keys": draw_keys(jax.random.fold_in(key_of[5], 71), 0),
        "values": scatter_about(key_of[2], (ROLLOUT_COUNT, ROLLOUT_LENGTH, KVW), 1.0, 6.0, ((0, 8), (1, 64))),
        "conv_taps": scatter_about(key_of[3], (TAPS, KVW), 0.5, 2.0, (), jnp.float32),
        "grad_out": draw_grad_out(jax.random.fold_in(key_of[5], 71), 0),
    }


NEG_FILL = -1e+30

def attend(query_block, grad_block, key_block, value_block, first_query, window):
    tok_rows = query_block.shape[0]
    keys_len = key_block.shape[0]
    kv_heads = key_block.shape[1] // HEAD_SIZE
    group_size = query_block.shape[1] // (HEAD_SIZE * kv_heads)
    inv_root = 1.0 / math.sqrt(HEAD_SIZE)
    query_pos = first_query + jnp.arange(tok_rows, dtype=jnp.int32)
    key_pos = first_query - window + jnp.arange(keys_len, dtype=jnp.int32)
    offset = query_pos[:, None] - key_pos[None, :]
    visible = (offset >= 0) & (offset < window) & (key_pos[None, :] >= 0)
    queries_grouped = query_block.reshape(tok_rows, kv_heads, group_size * HEAD_SIZE).transpose(1, 0, 2)
    grads_grouped = grad_block.reshape(tok_rows, kv_heads, group_size * HEAD_SIZE).transpose(1, 0, 2)
    keys_grouped = key_block.reshape(keys_len, kv_heads, HEAD_SIZE).transpose(1, 0, 2)
    values_grouped = value_block.reshape(keys_len, kv_heads, HEAD_SIZE).transpose(1, 0, 2)

    def one_group(operands):
        query_head, grad_head, key_head, value_head = operands
        query_head = query_head.reshape(tok_rows, group_size, HEAD_SIZE).astype(jnp.float32)
        grad_head = grad_head.reshape(tok_rows, group_size, HEAD_SIZE).astype(jnp.float32)
        key_wide = key_head.astype(jnp.float32)
        value_wide = value_head.astype(jnp.float32)
        scores = jnp.einsum('tgd,ld->gtl', query_head, key_wide) * inv_root
        scores = jnp.where(visible[None], scores, NEG_FILL)
        row_max = lax.optimization_barrier(jnp.max(scores, axis=-1, keepdims=True))
        row_sum = lax.optimization_barrier(jnp.sum(jnp.exp(scores - row_max), axis=-1, keepdims=True))
        log_total = row_max + jnp.log(row_sum)
        attn_prob = jnp.exp(scores - log_total)
        prob_low = attn_prob.astype(jnp.bfloat16)
        grad_prob = jnp.einsum('tgd,ld->gtl', grad_head, value_wide)
        row_delta = lax.optimization_barrier(jnp.sum(attn_prob * grad_prob, axis=-1, keepdims=True))
        grad_score = (attn_prob * (grad_prob - row_delta) * inv_root).astype(jnp.bfloat16)
        score_wide = grad_score.astype(jnp.float32)
        grad_query = jnp.einsum('gtl,ld->tgd', score_wide, key_wide).reshape(tok_rows, group_size * HEAD_SIZE)
        grad_key = jnp.einsum('gtl,tgd->ld', score_wide, query_head)
        grad_value = jnp.einsum('gtl,tgd->ld', prob_low.astype(jnp.float32), grad_head)
        return (grad_query, grad_key, grad_value)
    grad_query, grad_key, grad_value = lax.map(one_group, (queries_grouped, grads_grouped, keys_grouped, values_grouped))
    grad_query = grad_query.transpose(1, 0, 2).reshape(tok_rows, kv_heads * group_size * HEAD_SIZE)
    grad_key = grad_key.transpose(1, 0, 2).reshape(keys_len, kv_heads * HEAD_SIZE)
    grad_value = grad_value.transpose(1, 0, 2).reshape(keys_len, kv_heads * HEAD_SIZE)
    return (grad_query, grad_key, grad_value)

def reference(queries, keys, values, conv_taps, grad_out):
    seqs_count = queries.shape[0]
    rollout = queries.shape[1]
    kv_width = keys.shape[2]
    tap_count = conv_taps.shape[0]
    block_count = rollout // TOK_DEV

    def one_sequence(operands):
        query_seq, key_seq, value_seq, grad_seq = operands
        value_pad = jnp.pad(value_seq.astype(jnp.float32), ((tap_count - 1, 0), (0, 0)))
        summed = jnp.zeros((rollout, kv_width), jnp.float32)
        for index_k in range(tap_count):
            begin = tap_count - 1 - index_k
            summed = summed + conv_taps[index_k] * value_pad[begin:begin + rollout]
        mixed = summed.astype(jnp.bfloat16)
        key_pad = jnp.pad(key_seq, ((WINDOW, 0), (0, 0)))
        mixed_pad = jnp.pad(mixed, ((WINDOW, 0), (0, 0)))

        def one_block(carry, block_id):
            grad_keys_acc, grad_mixed_acc = carry
            start = (block_id * TOK_DEV).astype(jnp.int32)
            query_block = lax.dynamic_slice_in_dim(query_seq, start, TOK_DEV, 0)
            grad_block = lax.dynamic_slice_in_dim(grad_seq, start, TOK_DEV, 0)
            key_block = lax.dynamic_slice_in_dim(key_pad, start, WINDOW + TOK_DEV, 0)
            value_block = lax.dynamic_slice_in_dim(mixed_pad, start, WINDOW + TOK_DEV, 0)
            grad_query, grad_key, grad_value = attend(query_block, grad_block, key_block, value_block, start, WINDOW)
            old_keys = lax.dynamic_slice_in_dim(grad_keys_acc, start, WINDOW + TOK_DEV, 0)
            grad_keys_acc = lax.dynamic_update_slice_in_dim(grad_keys_acc, old_keys + grad_key, start, 0)
            old_mixed = lax.dynamic_slice_in_dim(grad_mixed_acc, start, WINDOW + TOK_DEV, 0)
            grad_mixed_acc = lax.dynamic_update_slice_in_dim(grad_mixed_acc, old_mixed + grad_value, start, 0)
            return ((grad_keys_acc, grad_mixed_acc), grad_query.astype(jnp.bfloat16))
        zeros_init = jnp.zeros((rollout + WINDOW, kv_width), jnp.float32)
        (grad_keys_acc, grad_mixed_acc), query_blocks = lax.scan(one_block, (zeros_init, zeros_init), jnp.arange(block_count, dtype=jnp.int32))
        grad_keys_seq = grad_keys_acc[WINDOW:]
        grad_mixed = grad_mixed_acc[WINDOW:]
        grad_pad = jnp.pad(grad_mixed, ((0, tap_count - 1), (0, 0)))
        grad_values_seq = jnp.zeros((rollout, kv_width), jnp.float32)
        tap_rows = []
        for index_k in range(tap_count):
            grad_values_seq = grad_values_seq + conv_taps[index_k] * grad_pad[index_k:index_k + rollout]
            begin = tap_count - 1 - index_k
            tap_rows.append(lax.optimization_barrier(jnp.sum(grad_mixed * value_pad[begin:begin + rollout], axis=0)))
        return (query_blocks.reshape(rollout, -1), grad_keys_seq.astype(jnp.bfloat16), grad_values_seq.astype(jnp.bfloat16), jnp.stack(tap_rows, axis=0))
    grad_queries, grad_keys, grad_values, tap_parts = lax.map(one_sequence, (queries, keys, values, grad_out))
    grad_taps = lax.optimization_barrier(jnp.sum(tap_parts, axis=0)).reshape(-1) / math.sqrt(seqs_count * rollout)
    return (grad_queries, grad_keys, grad_values, grad_taps)
```

```python
import math

import jax
import jax.numpy as jnp
from jax import lax
from jax.experimental import pallas as pl
from jax.experimental.pallas import tpu as pltpu
from jax.sharding import PartitionSpec as P

HEAD = 128
WINDOW = 1024
NEG_FILL = -1e30
F32 = jnp.float32
BF16 = jnp.bfloat16


def fdot(a, b):
    return lax.dot_general(a, b, (((1,), (0,)), ((), ())), preferred_element_type=F32)


def kernel(
    count,
    kv_heads,
    group,
    reach,
    rows,
    taps,
    q_ref,
    k_ref,
    v_ref,
    w_ref,
    g_ref,
    dq_ref,
    dk_ref,
    dv_ref,
    dw_ref,
    kv,
    kt,
    qs,
    qt,
    gs,
    gt,
    st,
    pt,
    ds,
    mx,
    stat,
    ret_in,
    ret_out,
    vext,
    gext,
    tail_in,
    head_in,
    fwd_send,
    fwd_recv,
    ret_send,
    ret_recv,
    edge_send,
    edge_recv,
):
    me = lax.axis_index("seq")
    right = lax.rem(me + 1, count)
    left = lax.rem(me + count - 1, count)
    wide = group * rows
    scale = 1.0 / math.sqrt(HEAD)
    log2_scale = scale * math.log2(math.e)

    barrier = pltpu.get_barrier_semaphore()
    for other in (left, right):
        pl.semaphore_signal(barrier, inc=1, device_id={"seq": other})
    pl.semaphore_wait(barrier, 2)

    def tail_copy():
        return pltpu.make_async_remote_copy(
            v_ref.at[pl.ds(rows - 16, 16)],
            tail_in,
            edge_send.at[0],
            edge_recv.at[0],
            device_id={"seq": right},
        )

    def head_copy():
        return pltpu.make_async_remote_copy(
            gext.at[pl.ds(0, 8)],
            head_in,
            edge_send.at[1],
            edge_recv.at[1],
            device_id={"seq": left},
        )

    def fwd_copy(j, h):
        return pltpu.make_async_remote_copy(
            kv.at[j - 1, h],
            kv.at[j, h],
            fwd_send.at[j - 1, h],
            fwd_recv.at[j - 1, h],
            device_id={"seq": right},
        )

    def ret_copy(j, h):
        return pltpu.make_async_remote_copy(
            ret_out.at[j - 1, h],
            ret_in.at[j - 1, h],
            ret_send.at[j - 1, h],
            ret_recv.at[j - 1, h],
            device_id={"seq": left},
        )

    tail_copy().start()
    vext[pl.ds(8, rows), :] = v_ref[...].astype(F32)
    for h in range(kv_heads):
        cols = slice(h * HEAD, (h + 1) * HEAD)
        kv[0, h, 0] = k_ref[:, cols]
    tail_copy().wait()
    tail = tail_in[pl.ds(8, 8), :].astype(F32)
    vext[pl.ds(0, 8), :] = jnp.where(me > 0, tail, jnp.zeros_like(tail))
    for h in range(kv_heads):
        cols = slice(h * HEAD, (h + 1) * HEAD)
        mixed = jnp.zeros((rows, HEAD), F32)
        for k in range(taps):
            mixed = mixed + w_ref[k : k + 1, cols] * vext[8 - k : 8 - k + rows, cols]
        kv[0, h, 1] = mixed.astype(BF16)
        fwd_copy(1, h).start()

    for h in range(kv_heads):
        for g in range(group):
            at = h * group + g
            qb = q_ref[:, at * HEAD : (at + 1) * HEAD]
            qs[h, g * rows : (g + 1) * rows, :] = qb
            qt[h, :, g * rows : (g + 1) * rows] = qb.T
            gb = g_ref[:, at * HEAD : (at + 1) * HEAD]
            gs[h, g * rows : (g + 1) * rows, :] = gb
            gt[h, :, g * rows : (g + 1) * rows] = gb.T

    key_at = lax.broadcasted_iota(jnp.int32, (rows, rows), 0)
    query_at = lax.broadcasted_iota(jnp.int32, (rows, rows), 1)

    def scores(j, h, mask, bias):
        kb = kv[j, h, 0]
        kt[h, j] = kb.T
        s = fdot(kb, qt[h])
        if mask is not None:
            s = jnp.where(jnp.concatenate([mask] * group, axis=1), s, NEG_FILL)
        if bias is not None:
            s = s + bias
        st[h, j] = s
        pt[h, j] = fdot(kv[j, h, 1], gt[h])
        top = jnp.max(s.reshape(rows // 8, 8, wide), axis=0)
        mx[h] = top if isinstance(j, int) and j == 0 else jnp.maximum(mx[h], top)

    for h in range(kv_heads):
        scores(0, h, query_at >= key_at, None)

    @pl.loop(1, reach)
    def _(j):
        bias = jnp.where(me >= j, 0.0, NEG_FILL).astype(F32)
        for h in range(kv_heads):
            fwd_copy(j, h).wait_recv()
            fwd_copy(j + 1, h).start()
            scores(j, h, None, bias)

    for h in range(kv_heads):
        fwd_copy(reach, h).wait_recv()
        bias = jnp.where(me >= reach, 0.0, NEG_FILL).astype(F32)
        scores(reach, h, query_at < key_at, bias)

    for h in range(kv_heads):
        top = jnp.max(mx[h], axis=0, keepdims=True)

        def body(j, carry):
            total, weighted = carry
            e = jnp.exp2((st[h, j] - top) * log2_scale)
            st[h, j] = e
            total = total + jnp.sum(e.reshape(rows // 8, 8, wide), axis=0)
            weighted = weighted + jnp.sum((e * pt[h, j]).reshape(rows // 8, 8, wide), axis=0)
            return total, weighted

        zero = jnp.zeros((8, wide), F32)
        total, weighted = lax.fori_loop(0, reach + 1, body, (zero, zero))
        inverse = 1.0 / jnp.sum(total, axis=0, keepdims=True)
        delta = jnp.sum(weighted, axis=0, keepdims=True) * inverse
        stat[h, 0:1, :] = inverse
        stat[h, 1:2, :] = delta

    def grads(j, h):
        p = st[h, j] * stat[h, 0:1, :]
        d = (p * (pt[h, j] - stat[h, 1:2, :]) * scale).astype(BF16)
        ds[h, j] = d
        return fdot(d, qs[h]), fdot(p.astype(BF16), gs[h])

    for h in range(kv_heads):
        dk, dv = grads(reach, h)
        ret_out[reach - 1, h, 0] = dk.astype(BF16)
        ret_out[reach - 1, h, 1] = dv.astype(BF16)
        ret_copy(reach, h).start()

    @pl.loop(1, reach)
    def _(i):
        j = reach - i
        for h in range(kv_heads):
            dk, dv = grads(j, h)
            ret_copy(j + 1, h).wait_recv()
            ret_out[j - 1, h, 0] = (dk + ret_in[j, h, 0].astype(F32)).astype(BF16)
            ret_out[j - 1, h, 1] = (dv + ret_in[j, h, 1].astype(F32)).astype(BF16)
            ret_copy(j, h).start()

    for h in range(kv_heads):
        cols = slice(h * HEAD, (h + 1) * HEAD)
        dk, dv = grads(0, h)
        ret_copy(1, h).wait_recv()
        dk_ref[:, cols] = (dk + ret_in[0, h, 0].astype(F32)).astype(BF16)
        gext[pl.ds(0, rows), cols] = dv + ret_in[0, h, 1].astype(F32)

    head_copy().start()
    for k in range(taps):
        product = gext[0:rows, :] * vext[8 - k : 8 - k + rows, :]
        dw_ref[k : k + 1, :] = jnp.sum(product, axis=0, keepdims=True)

    @pl.loop(0, kv_heads)
    def _(h):
        dq = fdot(kt[h, 0], ds[h, 0])
        for j in range(1, reach + 1):
            dq = dq + fdot(kt[h, j], ds[h, j])
        for g in range(group):
            block = dq[:, g * rows : (g + 1) * rows].T.astype(BF16)
            dq_ref[:, pl.ds(pl.multiple_of((h * group + g) * HEAD, HEAD), HEAD)] = block

    head_copy().wait()
    head = head_in[...]
    gext[pl.ds(rows, 8), :] = jnp.where(me < count - 1, head, jnp.zeros_like(head))
    total = jnp.zeros((rows, kv_heads * HEAD), F32)
    for k in range(taps):
        total = total + w_ref[k : k + 1, :] * gext[k : k + rows, :]
    dv_ref[...] = total.astype(BF16)

    @pl.loop(1, reach + 1)
    def _(j):
        for h in range(kv_heads):
            fwd_copy(j, h).wait_send()
            ret_copy(j, h).wait_send()


def on_device(queries, keys, values, conv_taps, grad_out):
    rows = queries.shape[1]
    taps = conv_taps.shape[0]
    width = keys.shape[2]
    kv_heads = width // HEAD
    group = queries.shape[2] // width
    reach = WINDOW // rows
    wide = group * rows
    count = lax.axis_size("seq")
    vmem = pl.BlockSpec(memory_space=pltpu.VMEM)

    def body(*refs):
        kernel(count, kv_heads, group, reach, rows, taps, *refs)

    dq, dk, dv, dw = pl.pallas_call(
        body,
        out_shape=(
            jax.ShapeDtypeStruct((rows, queries.shape[2]), BF16),
            jax.ShapeDtypeStruct((rows, width), BF16),
            jax.ShapeDtypeStruct((rows, width), BF16),
            jax.ShapeDtypeStruct((taps, width), F32),
        ),
        in_specs=[vmem] * 5,
        out_specs=(vmem,) * 4,
        scratch_shapes=[
            pltpu.VMEM((reach + 1, kv_heads, 2, rows, HEAD), BF16),
            pltpu.VMEM((kv_heads, reach + 1, HEAD, rows), BF16),
            pltpu.VMEM((kv_heads, wide, HEAD), BF16),
            pltpu.VMEM((kv_heads, HEAD, wide), BF16),
            pltpu.VMEM((kv_heads, wide, HEAD), BF16),
            pltpu.VMEM((kv_heads, HEAD, wide), BF16),
            pltpu.VMEM((kv_heads, reach + 1, rows, wide), F32),
            pltpu.VMEM((kv_heads, reach + 1, rows, wide), F32),
            pltpu.VMEM((kv_heads, reach + 1, rows, wide), BF16),
            pltpu.VMEM((kv_heads, 8, wide), F32),
            pltpu.VMEM((kv_heads, 8, wide), F32),
            pltpu.VMEM((reach, kv_heads, 2, rows, HEAD), BF16),
            pltpu.VMEM((reach, kv_heads, 2, rows, HEAD), BF16),
            pltpu.VMEM((rows + 8, width), F32),
            pltpu.VMEM((rows + 8, width), F32),
            pltpu.VMEM((16, width), BF16),
            pltpu.VMEM((8, width), F32),
            pltpu.SemaphoreType.DMA((reach, kv_heads)),
            pltpu.SemaphoreType.DMA((reach, kv_heads)),
            pltpu.SemaphoreType.DMA((reach, kv_heads)),
            pltpu.SemaphoreType.DMA((reach, kv_heads)),
            pltpu.SemaphoreType.DMA((2,)),
            pltpu.SemaphoreType.DMA((2,)),
        ],
        compiler_params=pltpu.CompilerParams(
            collective_id=0, has_side_effects=True, vmem_limit_bytes=56 * 1024 * 1024
        ),
        name="window_grads",
    )(queries[0], keys[0], values[0], conv_taps, grad_out[0])

    tokens = rows * count * lax.axis_size("rep")
    summed = lax.psum(dw.reshape(-1) * (1.0 / math.sqrt(tokens)), ("seq", "rep"))
    share = taps * width // count
    grad_taps = lax.dynamic_slice_in_dim(summed, lax.axis_index("seq") * share, share, 0)
    return dq[None], dk[None], dv[None], grad_taps


def solution(mesh):
    split = P("rep", "seq", None)
    return jax.shard_map(
        on_device,
        mesh=mesh,
        in_specs=(split, split, split, P(), split),
        out_specs=(split, split, split, P("seq")),
        check_vma=False,
    )
```

```python
import math

import jax
import jax.numpy as jnp
from jax import lax
from jax.experimental import pallas as pl
from jax.experimental.pallas import tpu as pltpu
from jax.sharding import PartitionSpec as P

HEAD = 128
WINDOW = 1024
NEG_FILL = -1e30
F32 = jnp.float32
BF16 = jnp.bfloat16


def fdot(a, b):
    return lax.dot_general(a, b, (((1,), (0,)), ((), ())), preferred_element_type=F32)


def kernel(
    count,
    rep_count,
    z_size,
    y_size,
    kv_heads,
    group,
    reach,
    rows,
    taps,
    q_ref,
    k_ref,
    v_ref,
    w_ref,
    g_ref,
    dq_ref,
    dk_ref,
    dv_ref,
    dw_ref,
    kv,
    kt,
    qs,
    qt,
    gs,
    gt,
    st,
    pt,
    ds,
    mx,
    stat,
    ret_in,
    ret_out,
    vext,
    gext,
    tail_in,
    head_in,
    fwd_send,
    fwd_recv,
    ret_send,
    ret_recv,
    edge_send,
    edge_recv,
    part,
    pair_in,
    part_pair,
    z_in,
    part_z,
    x_in,
    part_x,
    y_in,
    pair_send,
    pair_recv,
    z_send,
    z_recv,
    x_send,
    x_recv,
    y_send,
    y_recv,
):
    me = lax.axis_index("seq")
    rep = lax.axis_index("rep")
    right = lax.rem(me + 1, count)
    left = lax.rem(me + count - 1, count)
    wide = group * rows
    scale = 1.0 / math.sqrt(HEAD)
    log2_scale = scale * math.log2(math.e)

    z_at = lax.rem(lax.div(me, 2), z_size)
    partner = me + 1 - 2 * lax.rem(me, 2)
    across = lax.rem(me + count // 2, count)
    rep_pair = rep + 1 - 2 * lax.rem(rep, 2)
    x_peers = ((across, rep), (me, rep_pair), (across, rep_pair))

    def z_peer(i):
        z_to = lax.rem(z_at + i, z_size)
        return z_to, me + 2 * (z_to - z_at)

    def y_peer(i):
        return lax.rem(rep + 2 * i, rep_count)

    barrier = pltpu.get_barrier_semaphore()
    for other in (left, right):
        pl.semaphore_signal(barrier, inc=1, device_id={"seq": other})
    for x_seq, x_rep in x_peers:
        pl.semaphore_signal(barrier, inc=1, device_id={"seq": x_seq, "rep": x_rep})
    for i in range(1, y_size):
        pl.semaphore_signal(barrier, inc=1, device_id={"rep": y_peer(i)})

    @pl.loop(1, z_size)
    def _(i):
        pl.semaphore_signal(barrier, inc=1, device_id={"seq": z_peer(i)[1]})

    for h in range(kv_heads):
        for g in range(group):
            at = h * group + g
            qb = q_ref[:, at * HEAD : (at + 1) * HEAD]
            qs[h, g * rows : (g + 1) * rows, :] = qb
            qt[h, :, g * rows : (g + 1) * rows] = qb.T
            gb = g_ref[:, at * HEAD : (at + 1) * HEAD]
            gs[h, g * rows : (g + 1) * rows, :] = gb
            gt[h, :, g * rows : (g + 1) * rows] = gb.T
    vext[pl.ds(8, rows), :] = v_ref[...].astype(F32)
    for h in range(kv_heads):
        cols = slice(h * HEAD, (h + 1) * HEAD)
        kv[0, h, 0] = k_ref[:, cols]
    pl.semaphore_wait(barrier, 2 + len(x_peers) + y_size - 1 + z_size - 1)

    def pair_copy():
        return pltpu.make_async_remote_copy(
            part, pair_in, pair_send.at[0], pair_recv.at[0], device_id={"seq": partner}
        )

    def z_copy(i):
        z_to, seq_to = z_peer(i)
        return pltpu.make_async_remote_copy(
            part_pair.at[lax.div(z_to, 2)],
            z_in.at[i - 1],
            z_send.at[i - 1],
            z_recv.at[i - 1],
            device_id={"seq": seq_to},
        )

    def x_copy(i):
        x_seq, x_rep = x_peers[i]
        return pltpu.make_async_remote_copy(
            part_z, x_in.at[i], x_send.at[i], x_recv.at[i], device_id={"seq": x_seq, "rep": x_rep}
        )

    def y_copy(i):
        return pltpu.make_async_remote_copy(
            part_x,
            y_in.at[i - 1],
            y_send.at[i - 1],
            y_recv.at[i - 1],
            device_id={"rep": y_peer(i)},
        )

    def tail_copy():
        return pltpu.make_async_remote_copy(
            v_ref.at[pl.ds(rows - 16, 16)],
            tail_in,
            edge_send.at[0],
            edge_recv.at[0],
            device_id={"seq": right},
        )

    def head_copy():
        return pltpu.make_async_remote_copy(
            gext.at[pl.ds(0, 8)],
            head_in,
            edge_send.at[1],
            edge_recv.at[1],
            device_id={"seq": left},
        )

    def fwd_copy(j, h):
        return pltpu.make_async_remote_copy(
            kv.at[j - 1, h],
            kv.at[j, h],
            fwd_send.at[j - 1, h],
            fwd_recv.at[j - 1, h],
            device_id={"seq": right},
        )

    def ret_copy(j, h):
        return pltpu.make_async_remote_copy(
            ret_out.at[j - 1, h],
            ret_in.at[j - 1, h],
            ret_send.at[j - 1, h],
            ret_recv.at[j - 1, h],
            device_id={"seq": left},
        )

    tail_copy().start()
    tail_copy().wait()
    tail = tail_in[pl.ds(8, 8), :].astype(F32)
    vext[pl.ds(0, 8), :] = jnp.where(me > 0, tail, jnp.zeros_like(tail))
    for h in range(kv_heads):
        cols = slice(h * HEAD, (h + 1) * HEAD)
        mixed = jnp.zeros((rows, HEAD), F32)
        for k in range(taps):
            mixed = mixed + w_ref[k : k + 1, cols] * vext[8 - k : 8 - k + rows, cols]
        kv[0, h, 1] = mixed.astype(BF16)
        fwd_copy(1, h).start()

    key_at = lax.broadcasted_iota(jnp.int32, (rows, rows), 0)
    query_at = lax.broadcasted_iota(jnp.int32, (rows, rows), 1)

    def scores(j, h, mask, bias):
        kb = kv[j, h, 0]
        kt[h, j] = kb.T
        s = fdot(kb, qt[h])
        if mask is not None:
            s = jnp.where(jnp.concatenate([mask] * group, axis=1), s, NEG_FILL)
        if bias is not None:
            s = s + bias
        st[h, j] = s
        pt[h, j] = fdot(kv[j, h, 1], gt[h])
        top = jnp.max(s.reshape(rows // 8, 8, wide), axis=0)
        mx[h] = top if isinstance(j, int) and j == 0 else jnp.maximum(mx[h], top)

    for h in range(kv_heads):
        scores(0, h, query_at >= key_at, None)

    @pl.loop(1, reach)
    def _(j):
        bias = jnp.where(me >= j, 0.0, NEG_FILL).astype(F32)
        for h in range(kv_heads):
            fwd_copy(j, h).wait_recv()
            fwd_copy(j + 1, h).start()
            scores(j, h, None, bias)

    for h in range(kv_heads):
        fwd_copy(reach, h).wait_recv()
        bias = jnp.where(me >= reach, 0.0, NEG_FILL).astype(F32)
        scores(reach, h, query_at < key_at, bias)

    for h in range(kv_heads):
        top = jnp.max(mx[h], axis=0, keepdims=True)

        def body(j, carry):
            total, weighted = carry
            e = jnp.exp2((st[h, j] - top) * log2_scale)
            st[h, j] = e
            total = total + jnp.sum(e.reshape(rows // 8, 8, wide), axis=0)
            weighted = weighted + jnp.sum((e * pt[h, j]).reshape(rows // 8, 8, wide), axis=0)
            return total, weighted

        zero = jnp.zeros((8, wide), F32)
        total, weighted = lax.fori_loop(0, reach + 1, body, (zero, zero))
        inverse = 1.0 / jnp.sum(total, axis=0, keepdims=True)
        delta = jnp.sum(weighted, axis=0, keepdims=True) * inverse
        stat[h, 0:1, :] = inverse
        stat[h, 1:2, :] = delta

    def grads(j, h):
        p = st[h, j] * stat[h, 0:1, :]
        d = (p * (pt[h, j] - stat[h, 1:2, :]) * scale).astype(BF16)
        ds[h, j] = d
        return fdot(d, qs[h]), fdot(p.astype(BF16), gs[h])

    for h in range(kv_heads):
        dk, dv = grads(reach, h)
        ret_out[reach - 1, h, 0] = dk.astype(BF16)
        ret_out[reach - 1, h, 1] = dv.astype(BF16)
        ret_copy(reach, h).start()

    @pl.loop(1, reach)
    def _(i):
        j = reach - i
        for h in range(kv_heads):
            dk, dv = grads(j, h)
            ret_copy(j + 1, h).wait_recv()
            ret_out[j - 1, h, 0] = (dk + ret_in[j, h, 0].astype(F32)).astype(BF16)
            ret_out[j - 1, h, 1] = (dv + ret_in[j, h, 1].astype(F32)).astype(BF16)
            ret_copy(j, h).start()

    for h in range(kv_heads):
        cols = slice(h * HEAD, (h + 1) * HEAD)
        dk, dv = grads(0, h)
        ret_copy(1, h).wait_recv()
        dk_ref[:, cols] = (dk + ret_in[0, h, 0].astype(F32)).astype(BF16)
        gext[pl.ds(0, rows), cols] = dv + ret_in[0, h, 1].astype(F32)

    head_copy().start()
    for k in range(taps):
        product = gext[0:rows, :] * vext[8 - k : 8 - k + rows, :]
        summed = jnp.sum(product, axis=0, keepdims=True)
        for h in range(kv_heads):
            piece = (k % 2) * kv_heads + h
            part[piece, k // 2 : k // 2 + 1, :] = summed[:, h * HEAD : (h + 1) * HEAD]
    pair_copy().start()
    pair_copy().wait()
    part_pair[...] = part[...] + pair_in[...]

    @pl.loop(1, z_size)
    def _(i):
        z_copy(i).start()

    @pl.loop(0, kv_heads)
    def _(h):
        dq = fdot(kt[h, 0], ds[h, 0])
        for j in range(1, reach + 1):
            dq = dq + fdot(kt[h, j], ds[h, j])
        for g in range(group):
            block = dq[:, g * rows : (g + 1) * rows].T.astype(BF16)
            dq_ref[:, pl.ds(pl.multiple_of((h * group + g) * HEAD, HEAD), HEAD)] = block

    z_sum = part_pair[lax.div(z_at, 2)]
    for i in range(1, z_size):
        z_copy(i).wait_recv()
        z_sum = z_sum + z_in[i - 1]
    part_z[...] = z_sum
    for i in range(len(x_peers)):
        x_copy(i).start()

    head_copy().wait()
    head = head_in[...]
    gext[pl.ds(rows, 8), :] = jnp.where(me < count - 1, head, jnp.zeros_like(head))
    total = jnp.zeros((rows, kv_heads * HEAD), F32)
    for k in range(taps):
        total = total + w_ref[k : k + 1, :] * gext[k : k + rows, :]
    dv_ref[...] = total.astype(BF16)

    x_sum = part_z[...]
    for i in range(len(x_peers)):
        x_copy(i).wait_recv()
        x_sum = x_sum + x_in[i]
    part_x[...] = x_sum
    for i in range(1, y_size):
        y_copy(i).start()

    @pl.loop(1, reach + 1)
    def _(j):
        for h in range(kv_heads):
            fwd_copy(j, h).wait_send()
            ret_copy(j, h).wait_send()

    @pl.loop(1, z_size)
    def _(i):
        z_copy(i).wait_send()

    for i in range(len(x_peers)):
        x_copy(i).wait_send()
    y_sum = part_x[...]
    for i in range(1, y_size):
        y_copy(i).wait()
        y_sum = y_sum + y_in[i - 1]
    dw_ref[...] = y_sum * (1.0 / math.sqrt(rows * count * rep_count))


def on_device(queries, keys, values, conv_taps, grad_out):
    rows = queries.shape[1]
    taps = conv_taps.shape[0]
    width = keys.shape[2]
    kv_heads = width // HEAD
    group = queries.shape[2] // width
    reach = WINDOW // rows
    wide = group * rows
    count = lax.axis_size("seq")
    rep_count = lax.axis_size("rep")
    z_size = count // 4
    y_size = rep_count // 2
    pieces = z_size // 2
    vmem = pl.BlockSpec(memory_space=pltpu.VMEM)

    def body(*refs):
        kernel(count, rep_count, z_size, y_size, kv_heads, group, reach, rows, taps, *refs)

    dq, dk, dv, dw = pl.pallas_call(
        body,
        out_shape=(
            jax.ShapeDtypeStruct((rows, queries.shape[2]), BF16),
            jax.ShapeDtypeStruct((rows, width), BF16),
            jax.ShapeDtypeStruct((rows, width), BF16),
            jax.ShapeDtypeStruct((2, HEAD), F32),
        ),
        in_specs=[vmem] * 5,
        out_specs=(vmem,) * 4,
        scratch_shapes=[
            pltpu.VMEM((reach + 1, kv_heads, 2, rows, HEAD), BF16),
            pltpu.VMEM((kv_heads, reach + 1, HEAD, rows), BF16),
            pltpu.VMEM((kv_heads, wide, HEAD), BF16),
            pltpu.VMEM((kv_heads, HEAD, wide), BF16),
            pltpu.VMEM((kv_heads, wide, HEAD), BF16),
            pltpu.VMEM((kv_heads, HEAD, wide), BF16),
            pltpu.VMEM((kv_heads, reach + 1, rows, wide), F32),
            pltpu.VMEM((kv_heads, reach + 1, rows, wide), F32),
            pltpu.VMEM((kv_heads, reach + 1, rows, wide), BF16),
            pltpu.VMEM((kv_heads, 8, wide), F32),
            pltpu.VMEM((kv_heads, 8, wide), F32),
            pltpu.VMEM((reach, kv_heads, 2, rows, HEAD), BF16),
            pltpu.VMEM((reach, kv_heads, 2, rows, HEAD), BF16),
            pltpu.VMEM((rows + 8, width), F32),
            pltpu.VMEM((rows + 8, width), F32),
            pltpu.VMEM((16, width), BF16),
            pltpu.VMEM((8, width), F32),
            pltpu.SemaphoreType.DMA((reach, kv_heads)),
            pltpu.SemaphoreType.DMA((reach, kv_heads)),
            pltpu.SemaphoreType.DMA((reach, kv_heads)),
            pltpu.SemaphoreType.DMA((reach, kv_heads)),
            pltpu.SemaphoreType.DMA((2,)),
            pltpu.SemaphoreType.DMA((2,)),
            pltpu.VMEM((pieces, 2, HEAD), F32),
            pltpu.VMEM((pieces, 2, HEAD), F32),
            pltpu.VMEM((pieces, 2, HEAD), F32),
            pltpu.VMEM((z_size - 1, 2, HEAD), F32),
            pltpu.VMEM((2, HEAD), F32),
            pltpu.VMEM((3, 2, HEAD), F32),
            pltpu.VMEM((2, HEAD), F32),
            pltpu.VMEM((y_size - 1, 2, HEAD), F32),
            pltpu.SemaphoreType.DMA((1,)),
            pltpu.SemaphoreType.DMA((1,)),
            pltpu.SemaphoreType.DMA((z_size - 1,)),
            pltpu.SemaphoreType.DMA((z_size - 1,)),
            pltpu.SemaphoreType.DMA((3,)),
            pltpu.SemaphoreType.DMA((3,)),
            pltpu.SemaphoreType.DMA((y_size - 1,)),
            pltpu.SemaphoreType.DMA((y_size - 1,)),
        ],
        compiler_params=pltpu.CompilerParams(
            collective_id=0, has_side_effects=True, vmem_limit_bytes=56 * 1024 * 1024
        ),
        name="window_grads",
    )(queries[0], keys[0], values[0], conv_taps, grad_out[0])

    me = lax.axis_index("seq")
    share = taps * width // count
    at = (me // (count // 2), lax.rem(me, HEAD // share) * share)
    grad_taps = lax.dynamic_slice(dw, at, (1, share)).reshape(share)
    return dq[None], dk[None], dv[None], grad_taps


def solution(mesh):
    split = P("rep", "seq", None)
    return jax.shard_map(
        on_device,
        mesh=mesh,
        in_specs=(split, split, split, P(), split),
        out_specs=(split, split, split, P("seq")),
        check_vma=False,
    )
```

```python
import math

import jax
import jax.numpy as jnp
from jax import lax
from jax.experimental import pallas as pl
from jax.experimental.pallas import tpu as pltpu
from jax.sharding import PartitionSpec as P

HEAD = 128
WINDOW = 1024
NEG_FILL = -1e30
F32 = jnp.float32
BF16 = jnp.bfloat16


def fdot(a, b):
    return lax.dot_general(a, b, (((1,), (0,)), ((), ())), preferred_element_type=F32)


def kernel(
    count,
    rep_count,
    z_size,
    y_size,
    kv_heads,
    group,
    reach,
    rows,
    taps,
    q_ref,
    k_ref,
    v_ref,
    w_ref,
    g_ref,
    dq_ref,
    dk_ref,
    dv_ref,
    dw_ref,
    kv,
    kt,
    qs,
    qt,
    gs,
    gt,
    st,
    pt,
    ds,
    mx,
    stat,
    ret_in,
    ret_out,
    vx,
    gext,
    tail_in,
    own,
    tacc,
    head_in,
    fwd_send,
    fwd_recv,
    ret_send,
    ret_recv,
    edge_send,
    edge_recv,
    tail_send,
    tail_recv,
    part,
    pair_in,
    part_pair,
    z_in,
    part_z,
    x_in,
    part_x,
    y_in,
    pair_send,
    pair_recv,
    z_send,
    z_recv,
    x_send,
    x_recv,
    y_send,
    y_recv,
):
    me = lax.axis_index("seq")
    rep = lax.axis_index("rep")
    right = lax.rem(me + 1, count)
    left = lax.rem(me + count - 1, count)
    wide = group * rows
    scale = 1.0 / math.sqrt(HEAD)
    log2_scale = scale * math.log2(math.e)

    z_at = lax.rem(lax.div(me, 2), z_size)
    partner = me + 1 - 2 * lax.rem(me, 2)
    across = lax.rem(me + count // 2, count)
    rep_pair = rep + 1 - 2 * lax.rem(rep, 2)
    x_peers = ((across, rep), (me, rep_pair), (across, rep_pair))

    def z_peer(i):
        z_to = lax.rem(z_at + i, z_size)
        return z_to, me + 2 * (z_to - z_at)

    def y_peer(i):
        return lax.rem(rep + 2 * i, rep_count)

    barrier = pltpu.get_barrier_semaphore()
    for other in (left, right):
        pl.semaphore_signal(barrier, inc=1, device_id={"seq": other})
    for x_seq, x_rep in x_peers:
        pl.semaphore_signal(barrier, inc=1, device_id={"seq": x_seq, "rep": x_rep})
    for i in range(1, y_size):
        pl.semaphore_signal(barrier, inc=1, device_id={"rep": y_peer(i)})

    @pl.loop(1, z_size)
    def _(i):
        pl.semaphore_signal(barrier, inc=1, device_id={"seq": z_peer(i)[1]})

    for h in range(kv_heads):
        for g in range(group):
            at = h * group + g
            qb = q_ref[:, at * HEAD : (at + 1) * HEAD]
            qs[h, g * rows : (g + 1) * rows, :] = qb
            qt[h, :, g * rows : (g + 1) * rows] = qb.T
            gb = g_ref[:, at * HEAD : (at + 1) * HEAD]
            gs[h, g * rows : (g + 1) * rows, :] = gb
            gt[h, :, g * rows : (g + 1) * rows] = gb.T
    for h in range(kv_heads):
        cols = slice(h * HEAD, (h + 1) * HEAD)
        kv[0, h, 0] = k_ref[:, cols]
        kv[0, h, 1] = v_ref[:, cols]
    pl.semaphore_wait(barrier, 2 + len(x_peers) + y_size - 1 + z_size - 1)

    def pair_copy():
        return pltpu.make_async_remote_copy(
            part, pair_in, pair_send.at[0], pair_recv.at[0], device_id={"seq": partner}
        )

    def z_copy(i):
        z_to, seq_to = z_peer(i)
        return pltpu.make_async_remote_copy(
            part_pair.at[lax.div(z_to, 2)],
            z_in.at[i - 1],
            z_send.at[i - 1],
            z_recv.at[i - 1],
            device_id={"seq": seq_to},
        )

    def x_copy(i):
        x_seq, x_rep = x_peers[i]
        return pltpu.make_async_remote_copy(
            part_z, x_in.at[i], x_send.at[i], x_recv.at[i], device_id={"seq": x_seq, "rep": x_rep}
        )

    def y_copy(i):
        return pltpu.make_async_remote_copy(
            part_x,
            y_in.at[i - 1],
            y_send.at[i - 1],
            y_recv.at[i - 1],
            device_id={"rep": y_peer(i)},
        )

    def tail_copy(h):
        return pltpu.make_async_remote_copy(
            kv.at[reach, h, 1, pl.ds(rows - 16, 16)],
            tail_in.at[h],
            tail_send.at[h],
            tail_recv.at[h],
            device_id={"seq": right},
        )

    def head_copy():
        return pltpu.make_async_remote_copy(
            gext.at[pl.ds(0, 8)],
            head_in,
            edge_send.at[0],
            edge_recv.at[0],
            device_id={"seq": left},
        )

    def fwd_copy(j, h):
        return pltpu.make_async_remote_copy(
            kv.at[j - 1, h],
            kv.at[j, h],
            fwd_send.at[j - 1, h],
            fwd_recv.at[j - 1, h],
            device_id={"seq": right},
        )

    def ret_copy(j, h):
        return pltpu.make_async_remote_copy(
            ret_out.at[j - 1, h],
            ret_in.at[j - 1, h],
            ret_send.at[j - 1, h],
            ret_recv.at[j - 1, h],
            device_id={"seq": left},
        )

    key_at = lax.broadcasted_iota(jnp.int32, (rows, rows), 0)
    query_at = lax.broadcasted_iota(jnp.int32, (rows, rows), 1)

    def scores(j, h, mask, bias):
        kb = kv[j, h, 0]
        kt[h, j] = kb.T
        s = fdot(kb, qt[h])
        if mask is not None:
            s = jnp.where(jnp.concatenate([mask] * group, axis=1), s, NEG_FILL)
        if bias is not None:
            s = s + bias
        st[h, j] = s
        top = jnp.max(s.reshape(rows // 8, 8, wide), axis=0)
        mx[h] = top if isinstance(j, int) and j == 0 else jnp.maximum(mx[h], top)
        vx[h, j, pl.ds(8, rows), :] = kv[j, h, 1].astype(F32)

    def convolve(j, h, tail):
        tail = tail.astype(F32)[8:]
        vx[h, j, pl.ds(0, 8), :] = jnp.where(me > j, tail, jnp.zeros_like(tail))
        cols = slice(h * HEAD, (h + 1) * HEAD)
        mixed = jnp.zeros((rows, HEAD), F32)
        for k in range(taps):
            mixed = mixed + w_ref[k : k + 1, cols] * vx[h, j, pl.ds(8 - k, rows), :]
        pt[h, j] = fdot(mixed.astype(BF16), gt[h])

    def fwd_begin(h):
        fwd_copy(1, h).start()

    def fwd_step(j, h):
        fwd_copy(j, h).wait_recv()
        fwd_copy(j + 1, h).start()
        scores(j, h, None, jnp.where(me >= j, 0.0, NEG_FILL).astype(F32))
        convolve(j - 1, h, kv[j, h, 1, rows - 16 :, :])

    def fwd_last(h):
        fwd_copy(reach, h).wait_recv()
        tail_copy(h).start()
        bias = jnp.where(me >= reach, 0.0, NEG_FILL).astype(F32)
        scores(reach, h, query_at < key_at, bias)
        convolve(reach - 1, h, kv[reach, h, 1, rows - 16 :, :])

    def fwd_end(h):
        tail_copy(h).wait_recv()
        convolve(reach, h, tail_in[h])

    def stats(h):
        top = jnp.max(mx[h], axis=0, keepdims=True)

        def body(j, carry):
            total, weighted = carry
            e = jnp.exp2((st[h, j] - top) * log2_scale)
            st[h, j] = e
            total = total + jnp.sum(e.reshape(rows // 8, 8, wide), axis=0)
            weighted = weighted + jnp.sum((e * pt[h, j]).reshape(rows // 8, 8, wide), axis=0)
            return total, weighted

        zero = jnp.zeros((8, wide), F32)
        total, weighted = lax.fori_loop(0, reach + 1, body, (zero, zero))
        inverse = 1.0 / jnp.sum(total, axis=0, keepdims=True)
        delta = jnp.sum(weighted, axis=0, keepdims=True) * inverse
        stat[h, 0:1, :] = inverse
        stat[h, 1:2, :] = delta

    def grads(j, h):
        p = st[h, j] * stat[h, 0:1, :]
        d = (p * (pt[h, j] - stat[h, 1:2, :]) * scale).astype(BF16)
        ds[h, j] = d
        return fdot(d, qs[h]), fdot(p.astype(BF16), gs[h])

    def tap_sums(j, h, dv, fresh):
        for k in range(taps):
            product = dv * vx[h, j, pl.ds(8 - k, rows), :]
            product = jnp.sum(product.reshape(rows // 8, 8, HEAD), axis=0)
            tacc[h, k] = product if fresh else tacc[h, k] + product

    def ret_begin(heads):
        for h in heads:
            dk, dv = grads(reach, h)
            ret_out[reach - 1, h, 0] = dk.astype(BF16)
            ret_out[reach - 1, h, 1] = dv.astype(BF16)
            ret_copy(reach, h).start()
            tap_sums(reach, h, dv, True)

        @pl.loop(0, reach)
        def _(i):
            j = reach - 1 - i
            for h in heads:
                dk, dv = grads(j, h)
                own[h, j, 0] = dk
                own[h, j, 1] = dv
                tap_sums(j, h, dv, False)

    def ret_step(j, h):
        ret_copy(j + 1, h).wait_recv()
        for part_at in range(2):
            summed = own[h, j, part_at] + ret_in[j, h, part_at].astype(F32)
            ret_out[j - 1, h, part_at] = summed.astype(BF16)
        ret_copy(j, h).start()

    def ret_end(h):
        cols = slice(h * HEAD, (h + 1) * HEAD)
        ret_copy(1, h).wait_recv()
        dk_ref[:, cols] = (own[h, 0, 0] + ret_in[0, h, 0].astype(F32)).astype(BF16)
        gext[pl.ds(0, rows), cols] = own[h, 0, 1] + ret_in[0, h, 1].astype(F32)

    early = range(kv_heads // 2)
    late = range(kv_heads // 2, kv_heads)
    for h in early:
        fwd_begin(h)
    for h in range(kv_heads):
        scores(0, h, query_at >= key_at, None)

    @pl.loop(1, reach)
    def _(j):
        for h in early:
            fwd_step(j, h)

    for h in late:
        fwd_begin(h)
    for h in early:
        fwd_last(h)
    for h in early:
        fwd_end(h)
        stats(h)
    ret_begin(early)

    @pl.loop(1, reach)
    def _(j):
        for h in late:
            fwd_step(j, h)
        for h in early:
            ret_step(reach - j, h)

    for h in late:
        fwd_last(h)
    for h in early:
        ret_end(h)
    for h in late:
        fwd_end(h)
        stats(h)
    ret_begin(late)

    for h in range(kv_heads):
        for k in range(taps):
            piece = (k % 2) * kv_heads + h
            summed = jnp.sum(tacc[h, k], axis=0, keepdims=True)
            part[piece, k // 2 : k // 2 + 1, :] = summed
    pair_copy().start()

    def ret_span(first, last):
        @pl.loop(0, first - last + 1)
        def _(i):
            for h in late:
                ret_step(first - i, h)

    ret_span(reach - 1, reach - 1)
    pair_copy().wait()
    part_pair[...] = part[...] + pair_in[...]

    @pl.loop(1, z_size)
    def _(i):
        z_copy(i).start()

    ret_span(reach - 2, 3)
    z_sum = part_pair[lax.div(z_at, 2)]
    for i in range(1, z_size):
        z_copy(i).wait_recv()
        z_sum = z_sum + z_in[i - 1]
    part_z[...] = z_sum
    for i in range(len(x_peers)):
        x_copy(i).start()
    ret_span(2, 1)
    x_sum = part_z[...]
    for i in range(len(x_peers)):
        x_copy(i).wait_recv()
        x_sum = x_sum + x_in[i]
    part_x[...] = x_sum
    for i in range(1, y_size):
        y_copy(i).start()
    for h in late:
        ret_end(h)
    head_copy().start()

    @pl.loop(0, kv_heads)
    def _(h):
        dq = fdot(kt[h, 0], ds[h, 0])
        for j in range(1, reach + 1):
            dq = dq + fdot(kt[h, j], ds[h, j])
        for g in range(group):
            block = dq[:, g * rows : (g + 1) * rows].T.astype(BF16)
            dq_ref[:, pl.ds(pl.multiple_of((h * group + g) * HEAD, HEAD), HEAD)] = block

    head_copy().wait()
    head = head_in[...]
    gext[pl.ds(rows, 8), :] = jnp.where(me < count - 1, head, jnp.zeros_like(head))
    total = jnp.zeros((rows, kv_heads * HEAD), F32)
    for k in range(taps):
        total = total + w_ref[k : k + 1, :] * gext[k : k + rows, :]
    dv_ref[...] = total.astype(BF16)

    @pl.loop(1, reach + 1)
    def _(j):
        for h in range(kv_heads):
            fwd_copy(j, h).wait_send()
            ret_copy(j, h).wait_send()

    for h in range(kv_heads):
        tail_copy(h).wait_send()

    @pl.loop(1, z_size)
    def _(i):
        z_copy(i).wait_send()

    for i in range(len(x_peers)):
        x_copy(i).wait_send()
    y_sum = part_x[...]
    for i in range(1, y_size):
        y_copy(i).wait()
        y_sum = y_sum + y_in[i - 1]
    dw_ref[...] = y_sum * (1.0 / math.sqrt(rows * count * rep_count))


def on_device(queries, keys, values, conv_taps, grad_out):
    rows = queries.shape[1]
    taps = conv_taps.shape[0]
    width = keys.shape[2]
    kv_heads = width // HEAD
    group = queries.shape[2] // width
    reach = WINDOW // rows
    wide = group * rows
    count = lax.axis_size("seq")
    rep_count = lax.axis_size("rep")
    z_size = count // 4
    y_size = rep_count // 2
    pieces = z_size // 2
    vmem = pl.BlockSpec(memory_space=pltpu.VMEM)

    def body(*refs):
        kernel(count, rep_count, z_size, y_size, kv_heads, group, reach, rows, taps, *refs)

    dq, dk, dv, dw = pl.pallas_call(
        body,
        out_shape=(
            jax.ShapeDtypeStruct((rows, queries.shape[2]), BF16),
            jax.ShapeDtypeStruct((rows, width), BF16),
            jax.ShapeDtypeStruct((rows, width), BF16),
            jax.ShapeDtypeStruct((2, HEAD), F32),
        ),
        in_specs=[vmem] * 5,
        out_specs=(vmem,) * 4,
        scratch_shapes=[
            pltpu.VMEM((reach + 1, kv_heads, 2, rows, HEAD), BF16),
            pltpu.VMEM((kv_heads, reach + 1, HEAD, rows), BF16),
            pltpu.VMEM((kv_heads, wide, HEAD), BF16),
            pltpu.VMEM((kv_heads, HEAD, wide), BF16),
            pltpu.VMEM((kv_heads, wide, HEAD), BF16),
            pltpu.VMEM((kv_heads, HEAD, wide), BF16),
            pltpu.VMEM((kv_heads, reach + 1, rows, wide), F32),
            pltpu.VMEM((kv_heads, reach + 1, rows, wide), F32),
            pltpu.VMEM((kv_heads, reach + 1, rows, wide), BF16),
            pltpu.VMEM((kv_heads, 8, wide), F32),
            pltpu.VMEM((kv_heads, 8, wide), F32),
            pltpu.VMEM((reach, kv_heads, 2, rows, HEAD), BF16),
            pltpu.VMEM((reach, kv_heads, 2, rows, HEAD), BF16),
            pltpu.VMEM((kv_heads, reach + 1, rows + 8, HEAD), F32),
            pltpu.VMEM((rows + 8, width), F32),
            pltpu.VMEM((kv_heads, 16, HEAD), BF16),
            pltpu.VMEM((kv_heads, reach, 2, rows, HEAD), F32),
            pltpu.VMEM((kv_heads, taps, 8, HEAD), F32),
            pltpu.VMEM((8, width), F32),
            pltpu.SemaphoreType.DMA((reach, kv_heads)),
            pltpu.SemaphoreType.DMA((reach, kv_heads)),
            pltpu.SemaphoreType.DMA((reach, kv_heads)),
            pltpu.SemaphoreType.DMA((reach, kv_heads)),
            pltpu.SemaphoreType.DMA((1,)),
            pltpu.SemaphoreType.DMA((1,)),
            pltpu.SemaphoreType.DMA((kv_heads,)),
            pltpu.SemaphoreType.DMA((kv_heads,)),
            pltpu.VMEM((pieces, 2, HEAD), F32),
            pltpu.VMEM((pieces, 2, HEAD), F32),
            pltpu.VMEM((pieces, 2, HEAD), F32),
            pltpu.VMEM((z_size - 1, 2, HEAD), F32),
            pltpu.VMEM((2, HEAD), F32),
            pltpu.VMEM((3, 2, HEAD), F32),
            pltpu.VMEM((2, HEAD), F32),
            pltpu.VMEM((y_size - 1, 2, HEAD), F32),
            pltpu.SemaphoreType.DMA((1,)),
            pltpu.SemaphoreType.DMA((1,)),
            pltpu.SemaphoreType.DMA((z_size - 1,)),
            pltpu.SemaphoreType.DMA((z_size - 1,)),
            pltpu.SemaphoreType.DMA((3,)),
            pltpu.SemaphoreType.DMA((3,)),
            pltpu.SemaphoreType.DMA((y_size - 1,)),
            pltpu.SemaphoreType.DMA((y_size - 1,)),
        ],
        compiler_params=pltpu.CompilerParams(
            collective_id=0, has_side_effects=True, vmem_limit_bytes=56 * 1024 * 1024
        ),
        name="window_grads",
    )(queries[0], keys[0], values[0], conv_taps, grad_out[0])

    me = lax.axis_index("seq")
    share = taps * width // count
    at = (me // (count // 2), lax.rem(me, HEAD // share) * share)
    grad_taps = lax.dynamic_slice(dw, at, (1, share)).reshape(share)
    return dq[None], dk[None], dv[None], grad_taps


def solution(mesh):
    split = P("rep", "seq", None)
    return jax.shard_map(
        on_device,
        mesh=mesh,
        in_specs=(split, split, split, P(), split),
        out_specs=(split, split, split, P("seq")),
        check_vma=False,
    )
```

```python
import math

import jax
import jax.numpy as jnp
from jax import lax
from jax.experimental import pallas as pl
from jax.experimental.pallas import tpu as pltpu
from jax.sharding import PartitionSpec as P

HEAD = 128
WINDOW = 1024
NEG_FILL = -1e30
F32 = jnp.float32
BF16 = jnp.bfloat16


def fdot(a, b):
    return lax.dot_general(a, b, (((1,), (0,)), ((), ())), preferred_element_type=F32)


def kernel(
    count,
    rep_count,
    z_size,
    y_size,
    kv_heads,
    group,
    reach,
    rows,
    taps,
    q_ref,
    k_ref,
    v_ref,
    w_ref,
    g_ref,
    dq_ref,
    dk_ref,
    dv_ref,
    dw_ref,
    kv,
    kt,
    qs,
    qt,
    gs,
    gt,
    st,
    pt,
    ds,
    mx,
    stat,
    ret_in,
    ret_out,
    vx,
    gext,
    tail_in,
    own,
    tacc,
    head_in,
    fwd_send,
    fwd_recv,
    ret_send,
    ret_recv,
    share_send,
    share_recv,
    duo_in,
    duo_out,
    duo_send,
    duo_recv,
    edge_send,
    edge_recv,
    tail_send,
    tail_recv,
    part,
    pair_in,
    part_pair,
    z_in,
    part_z,
    x_in,
    part_x,
    y_in,
    pair_send,
    pair_recv,
    z_send,
    z_recv,
    x_send,
    x_recv,
    y_send,
    y_recv,
):
    me = lax.axis_index("seq")
    rep = lax.axis_index("rep")
    right = lax.rem(me + 1, count)
    left = lax.rem(me + count - 1, count)
    ahead = lax.rem(me + 2, count)
    behind = lax.rem(me + count - 2, count)
    core = lax.rem(me, 2)
    hops = reach // 2
    wide = group * rows
    scale = 1.0 / math.sqrt(HEAD)
    log2_scale = scale * math.log2(math.e)

    z_at = lax.rem(lax.div(me, 2), z_size)
    partner = me + 1 - 2 * lax.rem(me, 2)
    across = lax.rem(me + count // 2, count)
    rep_pair = rep + 1 - 2 * lax.rem(rep, 2)
    x_peers = ((across, rep), (me, rep_pair), (across, rep_pair))

    def z_peer(i):
        z_to = lax.rem(z_at + i, z_size)
        return z_to, me + 2 * (z_to - z_at)

    def y_peer(i):
        return lax.rem(rep + 2 * i, rep_count)

    barrier = pltpu.get_barrier_semaphore()
    far = (lax.rem(me + reach + 1, count), lax.rem(me + count - reach - 1, count))
    for other in (left, right, ahead, behind) + far:
        pl.semaphore_signal(barrier, inc=1, device_id={"seq": other})
    for x_seq, x_rep in x_peers:
        pl.semaphore_signal(barrier, inc=1, device_id={"seq": x_seq, "rep": x_rep})
    for i in range(1, y_size):
        pl.semaphore_signal(barrier, inc=1, device_id={"rep": y_peer(i)})

    @pl.loop(1, z_size)
    def _(i):
        pl.semaphore_signal(barrier, inc=1, device_id={"seq": z_peer(i)[1]})

    for h in range(kv_heads):
        for g in range(group):
            at = h * group + g
            qb = q_ref[:, at * HEAD : (at + 1) * HEAD]
            qs[h, g * rows : (g + 1) * rows, :] = qb
            qt[h, :, g * rows : (g + 1) * rows] = qb.T
            gb = g_ref[:, at * HEAD : (at + 1) * HEAD]
            gs[h, g * rows : (g + 1) * rows, :] = gb
            gt[h, :, g * rows : (g + 1) * rows] = gb.T
    for h in range(kv_heads):
        cols = slice(h * HEAD, (h + 1) * HEAD)
        kv[0, h, 0] = k_ref[:, cols]
        kv[0, h, 1] = v_ref[:, cols]
        for end in (0, hops + 1):
            duo_in[end, h] = jnp.zeros((2, rows, HEAD), BF16)
    pl.semaphore_wait(barrier, 6 + len(x_peers) + y_size - 1 + z_size - 1)

    def pair_copy():
        return pltpu.make_async_remote_copy(
            part, pair_in, pair_send.at[0], pair_recv.at[0], device_id={"seq": partner}
        )

    def z_copy(i):
        z_to, seq_to = z_peer(i)
        return pltpu.make_async_remote_copy(
            part_pair.at[lax.div(z_to, 2)],
            z_in.at[i - 1],
            z_send.at[i - 1],
            z_recv.at[i - 1],
            device_id={"seq": seq_to},
        )

    def x_copy(i):
        x_seq, x_rep = x_peers[i]
        return pltpu.make_async_remote_copy(
            part_z, x_in.at[i], x_send.at[i], x_recv.at[i], device_id={"seq": x_seq, "rep": x_rep}
        )

    def y_copy(i):
        return pltpu.make_async_remote_copy(
            part_x,
            y_in.at[i - 1],
            y_send.at[i - 1],
            y_recv.at[i - 1],
            device_id={"rep": y_peer(i)},
        )

    def tail_copy():
        return pltpu.make_async_remote_copy(
            v_ref.at[pl.ds(rows - 16, 16)],
            tail_in,
            tail_send.at[0],
            tail_recv.at[0],
            device_id={"seq": far[0]},
        )

    def head_copy():
        return pltpu.make_async_remote_copy(
            gext.at[pl.ds(0, 8)],
            head_in,
            edge_send.at[0],
            edge_recv.at[0],
            device_id={"seq": left},
        )

    def fwd_copy(t, h):
        return pltpu.make_async_remote_copy(
            kv.at[2 * t - 2, h],
            kv.at[2 * t, h],
            fwd_send.at[t - 1, h],
            fwd_recv.at[t - 1, h],
            device_id={"seq": ahead},
        )

    def share_copy(t, h):
        return pltpu.make_async_remote_copy(
            kv.at[2 * t - 2 + 2 * core, h],
            kv.at[2 * t - 1, h],
            share_send.at[t - 1, h],
            share_recv.at[t - 1, h],
            device_id={"seq": partner},
        )

    def duo_copy(m, h):
        return pltpu.make_async_remote_copy(
            duo_out.at[m, h],
            duo_in.at[m + 1, h],
            duo_send.at[m, h],
            duo_recv.at[m, h],
            device_id={"seq": partner},
        )

    def ret_copy(t, h):
        return pltpu.make_async_remote_copy(
            ret_out.at[t - 1, h],
            ret_in.at[t - 1, h],
            ret_send.at[t - 1, h],
            ret_recv.at[t - 1, h],
            device_id={"seq": behind},
        )

    key_at = lax.broadcasted_iota(jnp.int32, (rows, rows), 0)
    query_at = lax.broadcasted_iota(jnp.int32, (rows, rows), 1)

    def scores(j, h, mask, bias):
        kb = kv[j, h, 0]
        kt[h, j] = kb.T
        s = fdot(kb, qt[h])
        if mask is not None:
            s = jnp.where(jnp.concatenate([mask] * group, axis=1), s, NEG_FILL)
        if bias is not None:
            s = s + bias
        st[h, j] = s
        top = jnp.max(s.reshape(rows // 8, 8, wide), axis=0)
        mx[h] = top if isinstance(j, int) and j == 0 else jnp.maximum(mx[h], top)
        vx[h, j, pl.ds(8, rows), :] = kv[j, h, 1].astype(F32)

    def convolve(j, h, tail):
        tail = tail.astype(F32)[8:]
        vx[h, j, pl.ds(0, 8), :] = jnp.where(me > j, tail, jnp.zeros_like(tail))
        cols = slice(h * HEAD, (h + 1) * HEAD)
        mixed = jnp.zeros((rows, HEAD), F32)
        for k in range(taps):
            mixed = mixed + w_ref[k : k + 1, cols] * vx[h, j, pl.ds(8 - k, rows), :]
        pt[h, j] = fdot(mixed.astype(BF16), gt[h])

    def near(j, h):
        scores(j, h, None, jnp.where(me >= j, 0.0, NEG_FILL).astype(F32))

    def blend(j, h):
        convolve(j, h, kv[j + 1, h, 1, rows - 16 :, :])

    def fwd_begin(h):
        fwd_copy(1, h).start()

    def fwd_step(t, h):
        fwd_copy(t, h).wait_recv()
        if t < hops:
            fwd_copy(t + 1, h).start()
        share_copy(t, h).start()
        if t < hops:
            near(2 * t, h)
        else:
            bias = jnp.where(me >= reach, 0.0, NEG_FILL).astype(F32)
            scores(reach, h, query_at < key_at, bias)
        if t > 1:
            share_copy(t - 1, h).wait_recv()
            near(2 * t - 3, h)
            blend(2 * t - 4, h)
            blend(2 * t - 3, h)

    def fwd_end(h):
        share_copy(hops, h).wait_recv()
        near(reach - 1, h)
        blend(reach - 2, h)
        blend(reach - 1, h)
        convolve(reach, h, tail_in[:, h * HEAD : (h + 1) * HEAD])

    def stats(h):
        top = jnp.max(mx[h], axis=0, keepdims=True)

        def body(j, carry):
            total, weighted = carry
            e = jnp.exp2((st[h, j] - top) * log2_scale)
            st[h, j] = e
            total = total + jnp.sum(e.reshape(rows // 8, 8, wide), axis=0)
            weighted = weighted + jnp.sum((e * pt[h, j]).reshape(rows // 8, 8, wide), axis=0)
            return total, weighted

        zero = jnp.zeros((8, wide), F32)
        total, weighted = lax.fori_loop(0, reach + 1, body, (zero, zero))
        inverse = 1.0 / jnp.sum(total, axis=0, keepdims=True)
        delta = jnp.sum(weighted, axis=0, keepdims=True) * inverse
        stat[h, 0:1, :] = inverse
        stat[h, 1:2, :] = delta

    def grads(j, h):
        p = st[h, j] * stat[h, 0:1, :]
        d = (p * (pt[h, j] - stat[h, 1:2, :]) * scale).astype(BF16)
        ds[h, j] = d
        return fdot(d, qs[h]), fdot(p.astype(BF16), gs[h])

    def tap_sums(j, h, dv, fresh):
        for k in range(taps):
            product = dv * vx[h, j, pl.ds(8 - k, rows), :]
            product = jnp.sum(product.reshape(rows // 8, 8, HEAD), axis=0)
            tacc[h, k] = product if fresh else tacc[h, k] + product

    def odd_grads(m, h, fresh):
        dk, dv = grads(2 * m + 1, h)
        duo_out[m, h, 0] = dk.astype(BF16)
        duo_out[m, h, 1] = dv.astype(BF16)
        duo_copy(m, h).start()
        tap_sums(2 * m + 1, h, dv, fresh)

    def even_grads(t, h):
        dk, dv = grads(2 * t, h)
        own[h, t, 0] = dk
        own[h, t, 1] = dv
        tap_sums(2 * t, h, dv, False)

    def chip_sum(t, h, part_at):
        return own[h, t, part_at] + duo_in[t + 1 - core, h, part_at].astype(F32)

    def ret_begin(heads):
        for h in heads:
            odd_grads(hops - 1, h, True)
        for h in heads:
            even_grads(hops, h)
        for h in heads:
            duo_copy(hops - 1, h).wait_recv()
            for part_at in range(2):
                ret_out[hops - 1, h, part_at] = chip_sum(hops, h, part_at).astype(BF16)
            ret_copy(hops, h).start()

        @pl.loop(1, hops)
        def _(i):
            m = hops - 1 - i
            for h in heads:
                odd_grads(m, h, False)
            for h in heads:
                even_grads(m + 1, h)

        for h in heads:
            even_grads(0, h)

    def ret_step(t, h):
        ret_copy(t + 1, h).wait_recv()
        duo_copy(t - 1, h).wait_recv()
        for part_at in range(2):
            summed = chip_sum(t, h, part_at) + ret_in[t, h, part_at].astype(F32)
            ret_out[t - 1, h, part_at] = summed.astype(BF16)
        ret_copy(t, h).start()

    def ret_end(h):
        cols = slice(h * HEAD, (h + 1) * HEAD)
        ret_copy(1, h).wait_recv()
        dk_ref[:, cols] = (chip_sum(0, h, 0) + ret_in[0, h, 0].astype(F32)).astype(BF16)
        gext[pl.ds(0, rows), cols] = chip_sum(0, h, 1) + ret_in[0, h, 1].astype(F32)

    early = range(kv_heads // 2)
    late = range(kv_heads // 2, kv_heads)
    for h in early:
        fwd_begin(h)
    tail_copy().start()
    for h in range(kv_heads):
        scores(0, h, query_at >= key_at, None)
    for t in range(1, hops):
        for h in early:
            fwd_step(t, h)
    for h in late:
        fwd_begin(h)
    for h in early:
        fwd_step(hops, h)
    tail_copy().wait_recv()
    for h in early:
        fwd_end(h)
        stats(h)
    ret_begin(early)
    for t in range(1, hops + 1):
        for h in late:
            fwd_step(t, h)
        for h in early:
            if t < hops:
                ret_step(hops - t, h)
            else:
                ret_end(h)
    for h in late:
        fwd_end(h)
        stats(h)
    ret_begin(late)

    for h in range(kv_heads):
        for k in range(taps):
            piece = (k % 2) * kv_heads + h
            summed = jnp.sum(tacc[h, k], axis=0, keepdims=True)
            part[piece, k // 2 : k // 2 + 1, :] = summed
    pair_copy().start()

    for h in late:
        ret_step(hops - 1, h)
    pair_copy().wait()
    part_pair[...] = part[...] + pair_in[...]

    @pl.loop(1, z_size)
    def _(i):
        z_copy(i).start()

    for t in range(hops - 2, 0, -1):
        for h in late:
            ret_step(t, h)
    for h in late:
        ret_end(h)
    head_copy().start()
    z_sum = part_pair[lax.div(z_at, 2)]
    for i in range(1, z_size):
        z_copy(i).wait_recv()
        z_sum = z_sum + z_in[i - 1]
    part_z[...] = z_sum
    for i in range(len(x_peers)):
        x_copy(i).start()

    @pl.loop(0, kv_heads)
    def _(h):
        dq = fdot(kt[h, 0], ds[h, 0])
        for j in range(1, reach + 1):
            dq = dq + fdot(kt[h, j], ds[h, j])
        for g in range(group):
            block = dq[:, g * rows : (g + 1) * rows].T.astype(BF16)
            dq_ref[:, pl.ds(pl.multiple_of((h * group + g) * HEAD, HEAD), HEAD)] = block

    x_sum = part_z[...]
    for i in range(len(x_peers)):
        x_copy(i).wait_recv()
        x_sum = x_sum + x_in[i]
    part_x[...] = x_sum
    for i in range(1, y_size):
        y_copy(i).start()

    head_copy().wait()
    head = head_in[...]
    gext[pl.ds(rows, 8), :] = jnp.where(me < count - 1, head, jnp.zeros_like(head))
    total = jnp.zeros((rows, kv_heads * HEAD), F32)
    for k in range(taps):
        total = total + w_ref[k : k + 1, :] * gext[k : k + rows, :]
    dv_ref[...] = total.astype(BF16)

    @pl.loop(1, hops + 1)
    def _(t):
        for h in range(kv_heads):
            fwd_copy(t, h).wait_send()
            share_copy(t, h).wait_send()
            duo_copy(t - 1, h).wait_send()
            ret_copy(t, h).wait_send()

    tail_copy().wait_send()

    @pl.loop(1, z_size)
    def _(i):
        z_copy(i).wait_send()

    for i in range(len(x_peers)):
        x_copy(i).wait_send()
    y_sum = part_x[...]
    for i in range(1, y_size):
        y_copy(i).wait()
        y_sum = y_sum + y_in[i - 1]
    dw_ref[...] = y_sum * (1.0 / math.sqrt(rows * count * rep_count))


def on_device(queries, keys, values, conv_taps, grad_out):
    rows = queries.shape[1]
    taps = conv_taps.shape[0]
    width = keys.shape[2]
    kv_heads = width // HEAD
    group = queries.shape[2] // width
    reach = WINDOW // rows
    hops = reach // 2
    wide = group * rows
    count = lax.axis_size("seq")
    rep_count = lax.axis_size("rep")
    z_size = count // 4
    y_size = rep_count // 2
    pieces = z_size // 2
    vmem = pl.BlockSpec(memory_space=pltpu.VMEM)

    def body(*refs):
        kernel(count, rep_count, z_size, y_size, kv_heads, group, reach, rows, taps, *refs)

    dq, dk, dv, dw = pl.pallas_call(
        body,
        out_shape=(
            jax.ShapeDtypeStruct((rows, queries.shape[2]), BF16),
            jax.ShapeDtypeStruct((rows, width), BF16),
            jax.ShapeDtypeStruct((rows, width), BF16),
            jax.ShapeDtypeStruct((2, HEAD), F32),
        ),
        in_specs=[vmem] * 5,
        out_specs=(vmem,) * 4,
        scratch_shapes=[
            pltpu.VMEM((reach + 1, kv_heads, 2, rows, HEAD), BF16),
            pltpu.VMEM((kv_heads, reach + 1, HEAD, rows), BF16),
            pltpu.VMEM((kv_heads, wide, HEAD), BF16),
            pltpu.VMEM((kv_heads, HEAD, wide), BF16),
            pltpu.VMEM((kv_heads, wide, HEAD), BF16),
            pltpu.VMEM((kv_heads, HEAD, wide), BF16),
            pltpu.VMEM((kv_heads, reach + 1, rows, wide), F32),
            pltpu.VMEM((kv_heads, reach + 1, rows, wide), F32),
            pltpu.VMEM((kv_heads, reach + 1, rows, wide), BF16),
            pltpu.VMEM((kv_heads, 8, wide), F32),
            pltpu.VMEM((kv_heads, 8, wide), F32),
            pltpu.VMEM((hops, kv_heads, 2, rows, HEAD), BF16),
            pltpu.VMEM((hops, kv_heads, 2, rows, HEAD), BF16),
            pltpu.VMEM((kv_heads, reach + 1, rows + 8, HEAD), F32),
            pltpu.VMEM((rows + 8, width), F32),
            pltpu.VMEM((16, width), BF16),
            pltpu.VMEM((kv_heads, hops + 1, 2, rows, HEAD), F32),
            pltpu.VMEM((kv_heads, taps, 8, HEAD), F32),
            pltpu.VMEM((8, width), F32),
            pltpu.SemaphoreType.DMA((hops, kv_heads)),
            pltpu.SemaphoreType.DMA((hops, kv_heads)),
            pltpu.SemaphoreType.DMA((hops, kv_heads)),
            pltpu.SemaphoreType.DMA((hops, kv_heads)),
            pltpu.SemaphoreType.DMA((hops, kv_heads)),
            pltpu.SemaphoreType.DMA((hops, kv_heads)),
            pltpu.VMEM((hops + 2, kv_heads, 2, rows, HEAD), BF16),
            pltpu.VMEM((hops, kv_heads, 2, rows, HEAD), BF16),
            pltpu.SemaphoreType.DMA((hops, kv_heads)),
            pltpu.SemaphoreType.DMA((hops, kv_heads)),
            pltpu.SemaphoreType.DMA((1,)),
            pltpu.SemaphoreType.DMA((1,)),
            pltpu.SemaphoreType.DMA((1,)),
            pltpu.SemaphoreType.DMA((1,)),
            pltpu.VMEM((pieces, 2, HEAD), F32),
            pltpu.VMEM((pieces, 2, HEAD), F32),
            pltpu.VMEM((pieces, 2, HEAD), F32),
            pltpu.VMEM((z_size - 1, 2, HEAD), F32),
            pltpu.VMEM((2, HEAD), F32),
            pltpu.VMEM((3, 2, HEAD), F32),
            pltpu.VMEM((2, HEAD), F32),
            pltpu.VMEM((y_size - 1, 2, HEAD), F32),
            pltpu.SemaphoreType.DMA((1,)),
            pltpu.SemaphoreType.DMA((1,)),
            pltpu.SemaphoreType.DMA((z_size - 1,)),
            pltpu.SemaphoreType.DMA((z_size - 1,)),
            pltpu.SemaphoreType.DMA((3,)),
            pltpu.SemaphoreType.DMA((3,)),
            pltpu.SemaphoreType.DMA((y_size - 1,)),
            pltpu.SemaphoreType.DMA((y_size - 1,)),
        ],
        compiler_params=pltpu.CompilerParams(
            collective_id=0, has_side_effects=True, vmem_limit_bytes=56 * 1024 * 1024
        ),
        name="window_grads",
    )(queries[0], keys[0], values[0], conv_taps, grad_out[0])

    me = lax.axis_index("seq")
    share = taps * width // count
    at = (me // (count // 2), lax.rem(me, HEAD // share) * share)
    grad_taps = lax.dynamic_slice(dw, at, (1, share)).reshape(share)
    return dq[None], dk[None], dv[None], grad_taps


def solution(mesh):
    split = P("rep", "seq", None)
    return jax.shard_map(
        on_device,
        mesh=mesh,
        in_specs=(split, split, split, P(), split),
        out_specs=(split, split, split, P("seq")),
        check_vma=False,
    )
```

```python
import math

import jax
import jax.numpy as jnp
from jax import lax
from jax.experimental import pallas as pl
from jax.experimental.pallas import tpu as pltpu
from jax.sharding import PartitionSpec as P

HEAD = 128
WINDOW = 1024
NEG_FILL = -1e30
F32 = jnp.float32
BF16 = jnp.bfloat16


def fdot(a, b):
    return lax.dot_general(a, b, (((1,), (0,)), ((), ())), preferred_element_type=F32)


def kernel(
    count,
    rep_count,
    z_size,
    y_size,
    kv_heads,
    group,
    reach,
    rows,
    taps,
    q_ref,
    k_ref,
    v_ref,
    w_ref,
    g_ref,
    dq_ref,
    dk_ref,
    dv_ref,
    dw_ref,
    kv,
    kt,
    qs,
    qt,
    gs,
    gt,
    st,
    pt,
    ds,
    mx,
    stat,
    ret_in,
    ret_out,
    vx,
    gext,
    tail_in,
    own,
    tacc,
    head_in,
    fwd_send,
    fwd_recv,
    ret_send,
    ret_recv,
    share_send,
    share_recv,
    duo_in,
    duo_out,
    duo_send,
    duo_recv,
    edge_send,
    edge_recv,
    tail_send,
    tail_recv,
    part,
    pair_in,
    part_pair,
    z_in,
    part_z,
    x_in,
    part_x,
    y_in,
    pair_send,
    pair_recv,
    z_send,
    z_recv,
    x_send,
    x_recv,
    y_send,
    y_recv,
):
    me = lax.axis_index("seq")
    rep = lax.axis_index("rep")
    right = lax.rem(me + 1, count)
    left = lax.rem(me + count - 1, count)
    ahead = lax.rem(me + 2, count)
    behind = lax.rem(me + count - 2, count)
    core = lax.rem(me, 2)
    hops = reach // 2
    wide = group * rows
    scale = 1.0 / math.sqrt(HEAD)
    log2_scale = scale * math.log2(math.e)

    z_at = lax.rem(lax.div(me, 2), z_size)
    partner = me + 1 - 2 * lax.rem(me, 2)
    across = lax.rem(me + count // 2, count)
    rep_pair = rep + 1 - 2 * lax.rem(rep, 2)
    x_peers = ((across, rep), (me, rep_pair), (across, rep_pair))

    def z_peer(i):
        z_to = lax.rem(z_at + i, z_size)
        return z_to, me + 2 * (z_to - z_at)

    def y_peer(i):
        return lax.rem(rep + 2 * i, rep_count)

    barrier = pltpu.get_barrier_semaphore()
    far = (lax.rem(me + reach + 1, count), lax.rem(me + count - reach - 1, count))
    for other in (left, right, ahead, behind) + far:
        pl.semaphore_signal(barrier, inc=1, device_id={"seq": other})
    for x_seq, x_rep in x_peers:
        pl.semaphore_signal(barrier, inc=1, device_id={"seq": x_seq, "rep": x_rep})
    for i in range(1, y_size):
        pl.semaphore_signal(barrier, inc=1, device_id={"rep": y_peer(i)})

    @pl.loop(1, z_size)
    def _(i):
        pl.semaphore_signal(barrier, inc=1, device_id={"seq": z_peer(i)[1]})

    for h in range(kv_heads):
        cols = slice(h * HEAD, (h + 1) * HEAD)
        kv[0, h, 0] = k_ref[:, cols]
        kv[0, h, 1] = v_ref[:, cols]
    pl.semaphore_wait(barrier, 6 + len(x_peers) + y_size - 1 + z_size - 1)

    def pair_copy():
        return pltpu.make_async_remote_copy(
            part, pair_in, pair_send.at[0], pair_recv.at[0], device_id={"seq": partner}
        )

    def z_copy(i):
        z_to, seq_to = z_peer(i)
        return pltpu.make_async_remote_copy(
            part_pair.at[lax.div(z_to, 2)],
            z_in.at[i - 1],
            z_send.at[i - 1],
            z_recv.at[i - 1],
            device_id={"seq": seq_to},
        )

    def x_copy(i):
        x_seq, x_rep = x_peers[i]
        return pltpu.make_async_remote_copy(
            part_z, x_in.at[i], x_send.at[i], x_recv.at[i], device_id={"seq": x_seq, "rep": x_rep}
        )

    def y_copy(i):
        return pltpu.make_async_remote_copy(
            part_x,
            y_in.at[i - 1],
            y_send.at[i - 1],
            y_recv.at[i - 1],
            device_id={"rep": y_peer(i)},
        )

    def tail_copy():
        return pltpu.make_async_remote_copy(
            v_ref.at[pl.ds(rows - 16, 16)],
            tail_in,
            tail_send.at[0],
            tail_recv.at[0],
            device_id={"seq": far[0]},
        )

    def head_copy():
        return pltpu.make_async_remote_copy(
            gext.at[pl.ds(0, 8)],
            head_in,
            edge_send.at[0],
            edge_recv.at[0],
            device_id={"seq": left},
        )

    def fwd_copy(t, h):
        return pltpu.make_async_remote_copy(
            kv.at[2 * t - 2, h],
            kv.at[2 * t, h],
            fwd_send.at[t - 1, h],
            fwd_recv.at[t - 1, h],
            device_id={"seq": ahead},
        )

    def share_copy(t, h):
        return pltpu.make_async_remote_copy(
            kv.at[2 * t - 2 + 2 * core, h],
            kv.at[2 * t - 1, h],
            share_send.at[t - 1, h],
            share_recv.at[t - 1, h],
            device_id={"seq": partner},
        )

    def duo_copy(m, h):
        return pltpu.make_async_remote_copy(
            duo_out.at[m, h],
            duo_in.at[m + 1, h],
            duo_send.at[m, h],
            duo_recv.at[m, h],
            device_id={"seq": partner},
        )

    def ret_copy(t, h):
        return pltpu.make_async_remote_copy(
            ret_out.at[t - 1, h],
            ret_in.at[t - 1, h],
            ret_send.at[t - 1, h],
            ret_recv.at[t - 1, h],
            device_id={"seq": behind},
        )

    key_at = lax.broadcasted_iota(jnp.int32, (rows, rows), 0)
    query_at = lax.broadcasted_iota(jnp.int32, (rows, rows), 1)

    def scores(j, h, mask, bias):
        kb = kv[j, h, 0]
        kt[h, j] = kb.T
        s = fdot(kb, qt[h])
        if mask is not None:
            s = jnp.where(jnp.concatenate([mask] * group, axis=1), s, NEG_FILL)
        if bias is not None:
            s = s + bias
        st[h, j] = s
        top = jnp.max(s.reshape(rows // 8, 8, wide), axis=0)
        mx[h] = top if isinstance(j, int) and j == 0 else jnp.maximum(mx[h], top)
        vx[h, j, pl.ds(8, rows), :] = kv[j, h, 1].astype(F32)

    def convolve(j, h, tail):
        tail = tail.astype(F32)[8:]
        vx[h, j, pl.ds(0, 8), :] = jnp.where(me > j, tail, jnp.zeros_like(tail))
        cols = slice(h * HEAD, (h + 1) * HEAD)
        mixed = jnp.zeros((rows, HEAD), F32)
        for k in range(taps):
            mixed = mixed + w_ref[k : k + 1, cols] * vx[h, j, pl.ds(8 - k, rows), :]
        pt[h, j] = fdot(mixed.astype(BF16), gt[h])

    def near(j, h):
        scores(j, h, None, jnp.where(me >= j, 0.0, NEG_FILL).astype(F32))

    def blend(j, h):
        convolve(j, h, kv[j + 1, h, 1, rows - 16 :, :])

    def fwd_begin(h):
        fwd_copy(1, h).start()

    def fwd_step(t, h):
        fwd_copy(t, h).wait_recv()
        if t < hops:
            fwd_copy(t + 1, h).start()
        share_copy(t, h).start()
        if t < hops:
            near(2 * t, h)
        else:
            bias = jnp.where(me >= reach, 0.0, NEG_FILL).astype(F32)
            scores(reach, h, query_at < key_at, bias)
        if t > 1:
            share_copy(t - 1, h).wait_recv()
            near(2 * t - 3, h)
            blend(2 * t - 4, h)
            blend(2 * t - 3, h)

    def fwd_end(h):
        share_copy(hops, h).wait_recv()
        near(reach - 1, h)
        blend(reach - 2, h)
        blend(reach - 1, h)
        convolve(reach, h, tail_in[:, h * HEAD : (h + 1) * HEAD])

    def stats(h):
        top = jnp.max(mx[h], axis=0, keepdims=True)

        def body(j, carry):
            total, weighted = carry
            e = jnp.exp2((st[h, j] - top) * log2_scale)
            st[h, j] = e
            total = total + jnp.sum(e.reshape(rows // 8, 8, wide), axis=0)
            weighted = weighted + jnp.sum((e * pt[h, j]).reshape(rows // 8, 8, wide), axis=0)
            return total, weighted

        zero = jnp.zeros((8, wide), F32)
        total, weighted = lax.fori_loop(0, reach + 1, body, (zero, zero))
        inverse = 1.0 / jnp.sum(total, axis=0, keepdims=True)
        delta = jnp.sum(weighted, axis=0, keepdims=True) * inverse
        stat[h, 0:1, :] = inverse
        stat[h, 1:2, :] = delta

    def grads(j, h):
        p = st[h, j] * stat[h, 0:1, :]
        d = (p * (pt[h, j] - stat[h, 1:2, :]) * scale).astype(BF16)
        ds[h, j] = d
        return fdot(d, qs[h]), fdot(p.astype(BF16), gs[h])

    def tap_sums(j, h, dv, fresh):
        for k in range(taps):
            product = dv * vx[h, j, pl.ds(8 - k, rows), :]
            product = jnp.sum(product.reshape(rows // 8, 8, HEAD), axis=0)
            tacc[h, k] = product if fresh else tacc[h, k] + product

    def odd_grads(m, h, fresh):
        dk, dv = grads(2 * m + 1, h)
        duo_out[m, h, 0] = dk.astype(BF16)
        duo_out[m, h, 1] = dv.astype(BF16)
        duo_copy(m, h).start()
        tap_sums(2 * m + 1, h, dv, fresh)

    def even_grads(t, h):
        dk, dv = grads(2 * t, h)
        own[h, t, 0] = dk
        own[h, t, 1] = dv
        tap_sums(2 * t, h, dv, False)

    def chip_sum(t, h, part_at):
        return own[h, t, part_at] + duo_in[t + 1 - core, h, part_at].astype(F32)

    def ret_begin(heads):
        for h in heads:
            odd_grads(hops - 1, h, True)
        for h in heads:
            even_grads(hops, h)
        for h in heads:
            duo_copy(hops - 1, h).wait_recv()
            for part_at in range(2):
                ret_out[hops - 1, h, part_at] = chip_sum(hops, h, part_at).astype(BF16)
            ret_copy(hops, h).start()

        @pl.loop(1, hops)
        def _(i):
            m = hops - 1 - i
            for h in heads:
                odd_grads(m, h, False)
            for h in heads:
                even_grads(m + 1, h)

        for h in heads:
            even_grads(0, h)

    def ret_step(t, h):
        ret_copy(t + 1, h).wait_recv()
        duo_copy(t - 1, h).wait_recv()
        for part_at in range(2):
            summed = chip_sum(t, h, part_at) + ret_in[t, h, part_at].astype(F32)
            ret_out[t - 1, h, part_at] = summed.astype(BF16)
        ret_copy(t, h).start()

    def ret_end(h):
        cols = slice(h * HEAD, (h + 1) * HEAD)
        ret_copy(1, h).wait_recv()
        dk_ref[:, cols] = (chip_sum(0, h, 0) + ret_in[0, h, 0].astype(F32)).astype(BF16)
        gext[pl.ds(0, rows), cols] = chip_sum(0, h, 1) + ret_in[0, h, 1].astype(F32)

    early = range(kv_heads // 2)
    late = range(kv_heads // 2, kv_heads)
    for h in early:
        fwd_begin(h)
    tail_copy().start()
    for h in range(kv_heads):
        for g in range(group):
            at = h * group + g
            qb = q_ref[:, at * HEAD : (at + 1) * HEAD]
            qs[h, g * rows : (g + 1) * rows, :] = qb
            qt[h, :, g * rows : (g + 1) * rows] = qb.T
            gb = g_ref[:, at * HEAD : (at + 1) * HEAD]
            gs[h, g * rows : (g + 1) * rows, :] = gb
            gt[h, :, g * rows : (g + 1) * rows] = gb.T
    for h in range(kv_heads):
        for end in (0, hops + 1):
            duo_in[end, h] = jnp.zeros((2, rows, HEAD), BF16)
    for h in range(kv_heads):
        scores(0, h, query_at >= key_at, None)
    for t in range(1, hops + 1):
        for h in early:
            fwd_step(t, h)
        if t == 2:
            for h in late:
                fwd_begin(h)
        if t > 2:
            for h in late:
                fwd_step(t - 2, h)
    tail_copy().wait_recv()
    for h in early:
        fwd_end(h)
        stats(h)
    ret_begin(early)
    for t in range(3, hops + 1):
        for h in late:
            fwd_step(t, h)
        for h in early:
            ret_step(hops + 2 - t, h)
    for h in late:
        fwd_end(h)
        stats(h)
    ret_begin(late)

    for h in range(kv_heads):
        for k in range(taps):
            piece = (k % 2) * kv_heads + h
            summed = jnp.sum(tacc[h, k], axis=0, keepdims=True)
            part[piece, k // 2 : k // 2 + 1, :] = summed
    pair_copy().start()

    for h in early:
        ret_step(hops - 3, h)
    pair_copy().wait()
    part_pair[...] = part[...] + pair_in[...]

    @pl.loop(1, z_size)
    def _(i):
        z_copy(i).start()

    for h in late:
        ret_step(hops - 1, h)
    for h in early:
        ret_end(h)
    for t in range(hops - 2, 0, -1):
        for h in late:
            ret_step(t, h)
    z_sum = part_pair[lax.div(z_at, 2)]
    for i in range(1, z_size):
        z_copy(i).wait_recv()
        z_sum = z_sum + z_in[i - 1]
    part_z[...] = z_sum
    for i in range(len(x_peers)):
        x_copy(i).start()
    for h in late:
        ret_end(h)
    head_copy().start()
    x_sum = part_z[...]
    for i in range(len(x_peers)):
        x_copy(i).wait_recv()
        x_sum = x_sum + x_in[i]
    part_x[...] = x_sum
    for i in range(1, y_size):
        y_copy(i).start()

    @pl.loop(0, kv_heads)
    def _(h):
        dq = fdot(kt[h, 0], ds[h, 0])
        for j in range(1, reach + 1):
            dq = dq + fdot(kt[h, j], ds[h, j])
        for g in range(group):
            block = dq[:, g * rows : (g + 1) * rows].T.astype(BF16)
            dq_ref[:, pl.ds(pl.multiple_of((h * group + g) * HEAD, HEAD), HEAD)] = block

    head_copy().wait()
    head = head_in[...]
    gext[pl.ds(rows, 8), :] = jnp.where(me < count - 1, head, jnp.zeros_like(head))
    total = jnp.zeros((rows, kv_heads * HEAD), F32)
    for k in range(taps):
        total = total + w_ref[k : k + 1, :] * gext[k : k + rows, :]
    dv_ref[...] = total.astype(BF16)

    @pl.loop(1, hops + 1)
    def _(t):
        for h in range(kv_heads):
            fwd_copy(t, h).wait_send()
            share_copy(t, h).wait_send()
            duo_copy(t - 1, h).wait_send()
            ret_copy(t, h).wait_send()

    tail_copy().wait_send()

    @pl.loop(1, z_size)
    def _(i):
        z_copy(i).wait_send()

    for i in range(len(x_peers)):
        x_copy(i).wait_send()
    y_sum = part_x[...]
    for i in range(1, y_size):
        y_copy(i).wait()
        y_sum = y_sum + y_in[i - 1]
    dw_ref[...] = y_sum * (1.0 / math.sqrt(rows * count * rep_count))


def on_device(queries, keys, values, conv_taps, grad_out):
    rows = queries.shape[1]
    taps = conv_taps.shape[0]
    width = keys.shape[2]
    kv_heads = width // HEAD
    group = queries.shape[2] // width
    reach = WINDOW // rows
    hops = reach // 2
    wide = group * rows
    count = lax.axis_size("seq")
    rep_count = lax.axis_size("rep")
    z_size = count // 4
    y_size = rep_count // 2
    pieces = z_size // 2
    vmem = pl.BlockSpec(memory_space=pltpu.VMEM)

    def body(*refs):
        kernel(count, rep_count, z_size, y_size, kv_heads, group, reach, rows, taps, *refs)

    dq, dk, dv, dw = pl.pallas_call(
        body,
        out_shape=(
            jax.ShapeDtypeStruct((rows, queries.shape[2]), BF16),
            jax.ShapeDtypeStruct((rows, width), BF16),
            jax.ShapeDtypeStruct((rows, width), BF16),
            jax.ShapeDtypeStruct((2, HEAD), F32),
        ),
        in_specs=[vmem] * 5,
        out_specs=(vmem,) * 4,
        scratch_shapes=[
            pltpu.VMEM((reach + 1, kv_heads, 2, rows, HEAD), BF16),
            pltpu.VMEM((kv_heads, reach + 1, HEAD, rows), BF16),
            pltpu.VMEM((kv_heads, wide, HEAD), BF16),
            pltpu.VMEM((kv_heads, HEAD, wide), BF16),
            pltpu.VMEM((kv_heads, wide, HEAD), BF16),
            pltpu.VMEM((kv_heads, HEAD, wide), BF16),
            pltpu.VMEM((kv_heads, reach + 1, rows, wide), F32),
            pltpu.VMEM((kv_heads, reach + 1, rows, wide), F32),
            pltpu.VMEM((kv_heads, reach + 1, rows, wide), BF16),
            pltpu.VMEM((kv_heads, 8, wide), F32),
            pltpu.VMEM((kv_heads, 8, wide), F32),
            pltpu.VMEM((hops, kv_heads, 2, rows, HEAD), BF16),
            pltpu.VMEM((hops, kv_heads, 2, rows, HEAD), BF16),
            pltpu.VMEM((kv_heads, reach + 1, rows + 8, HEAD), F32),
            pltpu.VMEM((rows + 8, width), F32),
            pltpu.VMEM((16, width), BF16),
            pltpu.VMEM((kv_heads, hops + 1, 2, rows, HEAD), F32),
            pltpu.VMEM((kv_heads, taps, 8, HEAD), F32),
            pltpu.VMEM((8, width), F32),
            pltpu.SemaphoreType.DMA((hops, kv_heads)),
            pltpu.SemaphoreType.DMA((hops, kv_heads)),
            pltpu.SemaphoreType.DMA((hops, kv_heads)),
            pltpu.SemaphoreType.DMA((hops, kv_heads)),
            pltpu.SemaphoreType.DMA((hops, kv_heads)),
            pltpu.SemaphoreType.DMA((hops, kv_heads)),
            pltpu.VMEM((hops + 2, kv_heads, 2, rows, HEAD), BF16),
            pltpu.VMEM((hops, kv_heads, 2, rows, HEAD), BF16),
            pltpu.SemaphoreType.DMA((hops, kv_heads)),
            pltpu.SemaphoreType.DMA((hops, kv_heads)),
            pltpu.SemaphoreType.DMA((1,)),
            pltpu.SemaphoreType.DMA((1,)),
            pltpu.SemaphoreType.DMA((1,)),
            pltpu.SemaphoreType.DMA((1,)),
            pltpu.VMEM((pieces, 2, HEAD), F32),
            pltpu.VMEM((pieces, 2, HEAD), F32),
            pltpu.VMEM((pieces, 2, HEAD), F32),
            pltpu.VMEM((z_size - 1, 2, HEAD), F32),
            pltpu.VMEM((2, HEAD), F32),
            pltpu.VMEM((3, 2, HEAD), F32),
            pltpu.VMEM((2, HEAD), F32),
            pltpu.VMEM((y_size - 1, 2, HEAD), F32),
            pltpu.SemaphoreType.DMA((1,)),
            pltpu.SemaphoreType.DMA((1,)),
            pltpu.SemaphoreType.DMA((z_size - 1,)),
            pltpu.SemaphoreType.DMA((z_size - 1,)),
            pltpu.SemaphoreType.DMA((3,)),
            pltpu.SemaphoreType.DMA((3,)),
            pltpu.SemaphoreType.DMA((y_size - 1,)),
            pltpu.SemaphoreType.DMA((y_size - 1,)),
        ],
        compiler_params=pltpu.CompilerParams(
            collective_id=0, has_side_effects=True, vmem_limit_bytes=56 * 1024 * 1024
        ),
        name="window_grads",
    )(queries[0], keys[0], values[0], conv_taps, grad_out[0])

    me = lax.axis_index("seq")
    share = taps * width // count
    at = (me // (count // 2), lax.rem(me, HEAD // share) * share)
    grad_taps = lax.dynamic_slice(dw, at, (1, share)).reshape(share)
    return dq[None], dk[None], dv[None], grad_taps


def solution(mesh):
    split = P("rep", "seq", None)
    return jax.shard_map(
        on_device,
        mesh=mesh,
        in_specs=(split, split, split, P(), split),
        out_specs=(split, split, split, P("seq")),
        check_vma=False,
    )
```

```python
import math

import jax
import jax.numpy as jnp
from jax import lax
from jax.experimental import pallas as pl
from jax.experimental.pallas import tpu as pltpu
from jax.sharding import PartitionSpec as P

HEAD = 128
WINDOW = 1024
NEG_FILL = -1e30
F32 = jnp.float32
BF16 = jnp.bfloat16


def fdot(a, b):
    return lax.dot_general(a, b, (((1,), (0,)), ((), ())), preferred_element_type=F32)


def kernel(
    count,
    rep_count,
    z_size,
    y_size,
    kv_heads,
    group,
    reach,
    rows,
    taps,
    q_ref,
    k_ref,
    v_ref,
    w_ref,
    g_ref,
    dq_ref,
    dk_ref,
    dv_ref,
    dw_ref,
    kv,
    kt,
    qs,
    qt,
    gs,
    gt,
    st,
    pt,
    ds,
    mx,
    stat,
    ret_in,
    ret_out,
    vx,
    gext,
    tail_in,
    own,
    tacc,
    head_in,
    fwd_send,
    fwd_recv,
    ret_send,
    ret_recv,
    share_send,
    share_recv,
    duo_in,
    duo_out,
    duo_send,
    duo_recv,
    edge_send,
    edge_recv,
    tail_send,
    tail_recv,
    part,
    pair_in,
    part_pair,
    z_in,
    part_z,
    x_in,
    part_x,
    y_in,
    pair_send,
    pair_recv,
    z_send,
    z_recv,
    x_send,
    x_recv,
    y_send,
    y_recv,
):
    me = lax.axis_index("seq")
    rep = lax.axis_index("rep")
    right = lax.rem(me + 1, count)
    left = lax.rem(me + count - 1, count)
    ahead = lax.rem(me + 2, count)
    behind = lax.rem(me + count - 2, count)
    core = lax.rem(me, 2)
    hops = reach // 2
    wide = group * rows
    scale = 1.0 / math.sqrt(HEAD)
    log2_scale = scale * math.log2(math.e)

    z_at = lax.rem(lax.div(me, 2), z_size)
    partner = me + 1 - 2 * lax.rem(me, 2)
    across = lax.rem(me + count // 2, count)
    rep_pair = rep + 1 - 2 * lax.rem(rep, 2)
    x_peers = ((across, rep), (me, rep_pair), (across, rep_pair))

    def z_peer(i):
        z_to = lax.rem(z_at + i, z_size)
        return z_to, me + 2 * (z_to - z_at)

    def y_peer(i):
        return lax.rem(rep + 2 * i, rep_count)

    barrier = pltpu.get_barrier_semaphore()
    far = (lax.rem(me + reach + 1, count), lax.rem(me + count - reach - 1, count))
    for other in (left, right, ahead, behind) + far:
        pl.semaphore_signal(barrier, inc=1, device_id={"seq": other})
    for x_seq, x_rep in x_peers:
        pl.semaphore_signal(barrier, inc=1, device_id={"seq": x_seq, "rep": x_rep})
    for i in range(1, y_size):
        pl.semaphore_signal(barrier, inc=1, device_id={"rep": y_peer(i)})

    @pl.loop(1, z_size)
    def _(i):
        pl.semaphore_signal(barrier, inc=1, device_id={"seq": z_peer(i)[1]})

    for h in range(kv_heads):
        cols = slice(h * HEAD, (h + 1) * HEAD)
        kv[0, h, 0] = k_ref[:, cols]
        kv[0, h, 1] = v_ref[:, cols]
    pl.semaphore_wait(barrier, 6 + len(x_peers) + y_size - 1 + z_size - 1)

    def pair_copy():
        return pltpu.make_async_remote_copy(
            part, pair_in, pair_send.at[0], pair_recv.at[0], device_id={"seq": partner}
        )

    def z_copy(i):
        z_to, seq_to = z_peer(i)
        return pltpu.make_async_remote_copy(
            part_pair.at[lax.div(z_to, 2)],
            z_in.at[i - 1],
            z_send.at[i - 1],
            z_recv.at[i - 1],
            device_id={"seq": seq_to},
        )

    def x_copy(i):
        x_seq, x_rep = x_peers[i]
        return pltpu.make_async_remote_copy(
            part_z, x_in.at[i], x_send.at[i], x_recv.at[i], device_id={"seq": x_seq, "rep": x_rep}
        )

    def y_copy(i):
        return pltpu.make_async_remote_copy(
            part_x,
            y_in.at[i - 1],
            y_send.at[i - 1],
            y_recv.at[i - 1],
            device_id={"rep": y_peer(i)},
        )

    def tail_copy():
        return pltpu.make_async_remote_copy(
            v_ref.at[pl.ds(rows - 16, 16)],
            tail_in,
            tail_send.at[0],
            tail_recv.at[0],
            device_id={"seq": far[0]},
        )

    def head_copy():
        return pltpu.make_async_remote_copy(
            gext.at[pl.ds(0, 8)],
            head_in,
            edge_send.at[0],
            edge_recv.at[0],
            device_id={"seq": left},
        )

    def fwd_copy(t, h):
        return pltpu.make_async_remote_copy(
            kv.at[2 * t - 2, h],
            kv.at[2 * t, h],
            fwd_send.at[t - 1, h],
            fwd_recv.at[t - 1, h],
            device_id={"seq": ahead},
        )

    def share_copy(t, h):
        return pltpu.make_async_remote_copy(
            kv.at[2 * t - 2 + 2 * core, h],
            kv.at[2 * t - 1, h],
            share_send.at[t - 1, h],
            share_recv.at[t - 1, h],
            device_id={"seq": partner},
        )

    def duo_copy(m, h):
        return pltpu.make_async_remote_copy(
            duo_out.at[m, h],
            duo_in.at[m + 1, h],
            duo_send.at[m, h],
            duo_recv.at[m, h],
            device_id={"seq": partner},
        )

    def ret_copy(t, h):
        return pltpu.make_async_remote_copy(
            ret_out.at[t - 1, h],
            ret_in.at[t - 1, h],
            ret_send.at[t - 1, h],
            ret_recv.at[t - 1, h],
            device_id={"seq": behind},
        )

    key_at = lax.broadcasted_iota(jnp.int32, (rows, rows), 0)
    query_at = lax.broadcasted_iota(jnp.int32, (rows, rows), 1)

    def scores(j, h, mask, bias):
        kb = kv[j, h, 0]
        kt[h, j] = kb.T
        s = fdot(kb, qt[h])
        if mask is not None:
            s = jnp.where(jnp.concatenate([mask] * group, axis=1), s, NEG_FILL)
        if bias is not None:
            s = s + bias
        st[h, j] = s
        top = jnp.max(s.reshape(rows // 8, 8, wide), axis=0)
        mx[h] = top if isinstance(j, int) and j == 0 else jnp.maximum(mx[h], top)
        vx[h, j, pl.ds(8, rows), :] = kv[j, h, 1].astype(F32)

    def convolve(j, h, tail):
        tail = tail.astype(F32)[8:]
        vx[h, j, pl.ds(0, 8), :] = jnp.where(me > j, tail, jnp.zeros_like(tail))
        cols = slice(h * HEAD, (h + 1) * HEAD)
        mixed = jnp.zeros((rows, HEAD), F32)
        for k in range(taps):
            mixed = mixed + w_ref[k : k + 1, cols] * vx[h, j, pl.ds(8 - k, rows), :]
        pt[h, j] = fdot(mixed.astype(BF16), gt[h])

    def near(j, h):
        scores(j, h, None, jnp.where(me >= j, 0.0, NEG_FILL).astype(F32))

    def blend(j, h):
        convolve(j, h, kv[j + 1, h, 1, rows - 16 :, :])

    def fwd_begin(h):
        fwd_copy(1, h).start()

    def fwd_step(t, h):
        fwd_copy(t, h).wait_recv()
        if t < hops:
            fwd_copy(t + 1, h).start()
        share_copy(t, h).start()
        if t < hops:
            near(2 * t, h)
        else:
            bias = jnp.where(me >= reach, 0.0, NEG_FILL).astype(F32)
            scores(reach, h, query_at < key_at, bias)
        if t > 1:
            share_copy(t - 1, h).wait_recv()
            near(2 * t - 3, h)
            blend(2 * t - 4, h)
            blend(2 * t - 3, h)

    def fwd_end(h):
        share_copy(hops, h).wait_recv()
        near(reach - 1, h)
        blend(reach - 2, h)
        blend(reach - 1, h)
        convolve(reach, h, tail_in[:, h * HEAD : (h + 1) * HEAD])

    def stats(h):
        top = jnp.max(mx[h], axis=0, keepdims=True)

        def body(j, carry):
            total, weighted = carry
            e = jnp.exp2((st[h, j] - top) * log2_scale)
            st[h, j] = e
            total = total + jnp.sum(e.reshape(rows // 8, 8, wide), axis=0)
            weighted = weighted + jnp.sum((e * pt[h, j]).reshape(rows // 8, 8, wide), axis=0)
            return total, weighted

        zero = jnp.zeros((8, wide), F32)
        total, weighted = lax.fori_loop(0, reach + 1, body, (zero, zero))
        inverse = 1.0 / jnp.sum(total, axis=0, keepdims=True)
        delta = jnp.sum(weighted, axis=0, keepdims=True) * inverse
        stat[h, 0:1, :] = inverse
        stat[h, 1:2, :] = delta

    def grads(j, h):
        p = st[h, j] * stat[h, 0:1, :]
        d = (p * (pt[h, j] - stat[h, 1:2, :]) * scale).astype(BF16)
        ds[h, j] = d
        return fdot(d, qs[h]), fdot(p.astype(BF16), gs[h])

    def tap_sums(j, h, dv, fresh):
        for k in range(taps):
            product = dv * vx[h, j, pl.ds(8 - k, rows), :]
            product = jnp.sum(product.reshape(rows // 8, 8, HEAD), axis=0)
            tacc[h, k] = product if fresh else tacc[h, k] + product

    def odd_grads(m, h, fresh):
        dk, dv = grads(2 * m + 1, h)
        duo_out[m, h, 0] = dk.astype(BF16)
        duo_out[m, h, 1] = dv.astype(BF16)
        duo_copy(m, h).start()
        tap_sums(2 * m + 1, h, dv, fresh)

    def even_grads(t, h):
        dk, dv = grads(2 * t, h)
        own[h, t, 0] = dk
        own[h, t, 1] = dv
        tap_sums(2 * t, h, dv, False)

    def chip_sum(t, h, part_at):
        return own[h, t, part_at] + duo_in[t + 1 - core, h, part_at].astype(F32)

    def ret_begin(heads):
        for h in heads:
            odd_grads(hops - 1, h, True)
        for h in heads:
            even_grads(hops, h)
        for h in heads:
            duo_copy(hops - 1, h).wait_recv()
            for part_at in range(2):
                ret_out[hops - 1, h, part_at] = chip_sum(hops, h, part_at).astype(BF16)
            ret_copy(hops, h).start()

        @pl.loop(1, hops)
        def _(i):
            m = hops - 1 - i
            for h in heads:
                odd_grads(m, h, False)
            for h in heads:
                even_grads(m + 1, h)

        for h in heads:
            even_grads(0, h)

    def ret_step(t, h):
        ret_copy(t + 1, h).wait_recv()
        duo_copy(t - 1, h).wait_recv()
        for part_at in range(2):
            summed = chip_sum(t, h, part_at) + ret_in[t, h, part_at].astype(F32)
            ret_out[t - 1, h, part_at] = summed.astype(BF16)
        ret_copy(t, h).start()

    def ret_end(h):
        cols = slice(h * HEAD, (h + 1) * HEAD)
        ret_copy(1, h).wait_recv()
        dk_ref[:, cols] = (chip_sum(0, h, 0) + ret_in[0, h, 0].astype(F32)).astype(BF16)
        gext[pl.ds(0, rows), cols] = chip_sum(0, h, 1) + ret_in[0, h, 1].astype(F32)

    early = range(kv_heads // 2)
    late = range(kv_heads // 2, kv_heads)
    for h in early:
        fwd_begin(h)
    tail_copy().start()
    for h in range(kv_heads):
        for g in range(group):
            at = h * group + g
            qb = q_ref[:, at * HEAD : (at + 1) * HEAD]
            qs[h, g * rows : (g + 1) * rows, :] = qb
            qt[h, :, g * rows : (g + 1) * rows] = qb.T
            gb = g_ref[:, at * HEAD : (at + 1) * HEAD]
            gs[h, g * rows : (g + 1) * rows, :] = gb
            gt[h, :, g * rows : (g + 1) * rows] = gb.T
    for h in range(kv_heads):
        for end in (0, hops + 1):
            duo_in[end, h] = jnp.zeros((2, rows, HEAD), BF16)
    for h in range(kv_heads):
        scores(0, h, query_at >= key_at, None)
    for t in range(1, hops + 1):
        for h in early:
            fwd_step(t, h)
        if t == 1:
            for h in late:
                fwd_begin(h)
        if t > 1:
            for h in late:
                fwd_step(t - 1, h)
    tail_copy().wait_recv()
    for h in early:
        fwd_end(h)
        stats(h)
    ret_begin(early)
    for h in late:
        fwd_step(hops, h)
    for h in early:
        ret_step(hops - 1, h)
    for h in late:
        fwd_end(h)
        stats(h)
    ret_begin(late)

    for h in range(kv_heads):
        for k in range(taps):
            piece = (k % 2) * kv_heads + h
            summed = jnp.sum(tacc[h, k], axis=0, keepdims=True)
            part[piece, k // 2 : k // 2 + 1, :] = summed
    pair_copy().start()

    for h in early:
        ret_step(hops - 2, h)
    pair_copy().wait()
    part_pair[...] = part[...] + pair_in[...]

    @pl.loop(1, z_size)
    def _(i):
        z_copy(i).start()

    for t in range(hops - 1, 0, -1):
        for h in late:
            ret_step(t, h)
        for h in early:
            if t == hops - 1:
                ret_step(1, h)
            elif t == hops - 2:
                ret_end(h)
    z_sum = part_pair[lax.div(z_at, 2)]
    for i in range(1, z_size):
        z_copy(i).wait_recv()
        z_sum = z_sum + z_in[i - 1]
    part_z[...] = z_sum
    for i in range(len(x_peers)):
        x_copy(i).start()
    for h in late:
        ret_end(h)
    head_copy().start()
    x_sum = part_z[...]
    for i in range(len(x_peers)):
        x_copy(i).wait_recv()
        x_sum = x_sum + x_in[i]
    part_x[...] = x_sum
    for i in range(1, y_size):
        y_copy(i).start()

    @pl.loop(0, kv_heads)
    def _(h):
        dq = fdot(kt[h, 0], ds[h, 0])
        for j in range(1, reach + 1):
            dq = dq + fdot(kt[h, j], ds[h, j])
        for g in range(group):
            block = dq[:, g * rows : (g + 1) * rows].T.astype(BF16)
            dq_ref[:, pl.ds(pl.multiple_of((h * group + g) * HEAD, HEAD), HEAD)] = block

    head_copy().wait()
    head = head_in[...]
    gext[pl.ds(rows, 8), :] = jnp.where(me < count - 1, head, jnp.zeros_like(head))
    total = jnp.zeros((rows, kv_heads * HEAD), F32)
    for k in range(taps):
        total = total + w_ref[k : k + 1, :] * gext[k : k + rows, :]
    dv_ref[...] = total.astype(BF16)

    @pl.loop(1, hops + 1)
    def _(t):
        for h in range(kv_heads):
            fwd_copy(t, h).wait_send()
            share_copy(t, h).wait_send()
            duo_copy(t - 1, h).wait_send()
            ret_copy(t, h).wait_send()

    tail_copy().wait_send()

    @pl.loop(1, z_size)
    def _(i):
        z_copy(i).wait_send()

    for i in range(len(x_peers)):
        x_copy(i).wait_send()
    y_sum = part_x[...]
    for i in range(1, y_size):
        y_copy(i).wait()
        y_sum = y_sum + y_in[i - 1]
    dw_ref[...] = y_sum * (1.0 / math.sqrt(rows * count * rep_count))


def on_device(queries, keys, values, conv_taps, grad_out):
    rows = queries.shape[1]
    taps = conv_taps.shape[0]
    width = keys.shape[2]
    kv_heads = width // HEAD
    group = queries.shape[2] // width
    reach = WINDOW // rows
    hops = reach // 2
    wide = group * rows
    count = lax.axis_size("seq")
    rep_count = lax.axis_size("rep")
    z_size = count // 4
    y_size = rep_count // 2
    pieces = z_size // 2
    vmem = pl.BlockSpec(memory_space=pltpu.VMEM)

    def body(*refs):
        kernel(count, rep_count, z_size, y_size, kv_heads, group, reach, rows, taps, *refs)

    dq, dk, dv, dw = pl.pallas_call(
        body,
        out_shape=(
            jax.ShapeDtypeStruct((rows, queries.shape[2]), BF16),
            jax.ShapeDtypeStruct((rows, width), BF16),
            jax.ShapeDtypeStruct((rows, width), BF16),
            jax.ShapeDtypeStruct((2, HEAD), F32),
        ),
        in_specs=[vmem] * 5,
        out_specs=(vmem,) * 4,
        scratch_shapes=[
            pltpu.VMEM((reach + 1, kv_heads, 2, rows, HEAD), BF16),
            pltpu.VMEM((kv_heads, reach + 1, HEAD, rows), BF16),
            pltpu.VMEM((kv_heads, wide, HEAD), BF16),
            pltpu.VMEM((kv_heads, HEAD, wide), BF16),
            pltpu.VMEM((kv_heads, wide, HEAD), BF16),
            pltpu.VMEM((kv_heads, HEAD, wide), BF16),
            pltpu.VMEM((kv_heads, reach + 1, rows, wide), F32),
            pltpu.VMEM((kv_heads, reach + 1, rows, wide), F32),
            pltpu.VMEM((kv_heads, reach + 1, rows, wide), BF16),
            pltpu.VMEM((kv_heads, 8, wide), F32),
            pltpu.VMEM((kv_heads, 8, wide), F32),
            pltpu.VMEM((hops, kv_heads, 2, rows, HEAD), BF16),
            pltpu.VMEM((hops, kv_heads, 2, rows, HEAD), BF16),
            pltpu.VMEM((kv_heads, reach + 1, rows + 8, HEAD), F32),
            pltpu.VMEM((rows + 8, width), F32),
            pltpu.VMEM((16, width), BF16),
            pltpu.VMEM((kv_heads, hops + 1, 2, rows, HEAD), F32),
            pltpu.VMEM((kv_heads, taps, 8, HEAD), F32),
            pltpu.VMEM((8, width), F32),
            pltpu.SemaphoreType.DMA((hops, kv_heads)),
            pltpu.SemaphoreType.DMA((hops, kv_heads)),
            pltpu.SemaphoreType.DMA((hops, kv_heads)),
            pltpu.SemaphoreType.DMA((hops, kv_heads)),
            pltpu.SemaphoreType.DMA((hops, kv_heads)),
            pltpu.SemaphoreType.DMA((hops, kv_heads)),
            pltpu.VMEM((hops + 2, kv_heads, 2, rows, HEAD), BF16),
            pltpu.VMEM((hops, kv_heads, 2, rows, HEAD), BF16),
            pltpu.SemaphoreType.DMA((hops, kv_heads)),
            pltpu.SemaphoreType.DMA((hops, kv_heads)),
            pltpu.SemaphoreType.DMA((1,)),
            pltpu.SemaphoreType.DMA((1,)),
            pltpu.SemaphoreType.DMA((1,)),
            pltpu.SemaphoreType.DMA((1,)),
            pltpu.VMEM((pieces, 2, HEAD), F32),
            pltpu.VMEM((pieces, 2, HEAD), F32),
            pltpu.VMEM((pieces, 2, HEAD), F32),
            pltpu.VMEM((z_size - 1, 2, HEAD), F32),
            pltpu.VMEM((2, HEAD), F32),
            pltpu.VMEM((3, 2, HEAD), F32),
            pltpu.VMEM((2, HEAD), F32),
            pltpu.VMEM((y_size - 1, 2, HEAD), F32),
            pltpu.SemaphoreType.DMA((1,)),
            pltpu.SemaphoreType.DMA((1,)),
            pltpu.SemaphoreType.DMA((z_size - 1,)),
            pltpu.SemaphoreType.DMA((z_size - 1,)),
            pltpu.SemaphoreType.DMA((3,)),
            pltpu.SemaphoreType.DMA((3,)),
            pltpu.SemaphoreType.DMA((y_size - 1,)),
            pltpu.SemaphoreType.DMA((y_size - 1,)),
        ],
        compiler_params=pltpu.CompilerParams(
            collective_id=0, has_side_effects=True, vmem_limit_bytes=56 * 1024 * 1024
        ),
        name="window_grads",
    )(queries[0], keys[0], values[0], conv_taps, grad_out[0])

    me = lax.axis_index("seq")
    share = taps * width // count
    at = (me // (count // 2), lax.rem(me, HEAD // share) * share)
    grad_taps = lax.dynamic_slice(dw, at, (1, share)).reshape(share)
    return dq[None], dk[None], dv[None], grad_taps


def solution(mesh):
    split = P("rep", "seq", None)
    return jax.shard_map(
        on_device,
        mesh=mesh,
        in_specs=(split, split, split, P(), split),
        out_specs=(split, split, split, P("seq")),
        check_vma=False,
    )
```
